32 devices in a mesh: dp: 4 (over z), ctx: 8 (over y, x, core).
Axes of the slice: x: 2, y: 2, z: 4, core: 2. Of those that a mesh axis runs over, the one named last changes fastest.
Arguments:
- frames: bfloat16 [32, 2, 512, 512], P(('dp', 'ctx')), parts along dimension 0, may hold values from -6 to 6
- episode_lengths: int32 [64], P('dp'), parts along dimension 0, may hold values from 1 to 1024, 8192 in all
- w_qkv: bfloat16 [512, 1536], replicated, may hold values from -1 to 1
- w_out: bfloat16 [512, 512], replicated, may hold values from -0.25 to 0.25
Outputs:
- attended: bfloat16 [32, 2, 512, 512], P(('dp', 'ctx')), parts along dimension 0
The draws below stay inside these ranges and needn't reach their ends.
There are 4 independent parts, one for each index of `dp`. The reference program is written for one: setup_inputs(seed, part) draws one part's arguments, and reference() takes and returns one part's arrays. A program takes and returns all parts, laid end to end along the dimension named above; an argument that names none is the same for every part. Nothing has to cross between parts.
Inputs may be any that keep to these rules, and one draw needn't show every extreme that they name: `episode_lengths`: the lengths sum to 8192; the longest is exactly 1024 tokens.
All inputs are finite; a program needn't handle non-finite values.
Results may differ from the reference program's by a relative error of at most 0.0082.
Values may be sent and summed in bfloat16 or wider, within the bound.
No kernel may reach another device: no remote copies, remote signals or barrier semaphores. Data moves between devices by JAX's collectives and lax.ppermute only.
A program may use at most 64 MiB of HBM per device.

```python
import math
import jax
import jax.numpy as jnp
import numpy as np
from jax import lax

D = 512
HEADS = 4
HEAD_DIM = 128
CH = 512
WIN = 2
SEQ = 8192
EPI_MAX = 1024
EPISODES = 16
N_CTX = 8


def draw_frames(key, part):
    shape = (N_CTX, 2, CH, D)
    noise = jax.random.truncated_normal(key, -4.0, 4.0, shape, jnp.float32)
    return noise.astype(jnp.bfloat16)


def draw_w_qkv(key, part):
    base = jax.random.truncated_normal(key, -4.0, 4.0, (D, 3 * D), jnp.float32) * D ** (-0.5)
    return base.astype(jnp.bfloat16)


def length_profile(count, total, limit, lean):
    portions = [(1 << 20) // math.isqrt(standing ** lean) + 1 for standing in range(2, count + 1)]
    surplus, given = total - limit - (count - 1), [1] * (count - 1)
    while surplus > 0:
        movable = [i for i in range(count - 1) if given[i] < limit]
        mass, budget = sum([portions[i] for i in movable]), surplus
        for i in movable:
            extra = min(limit - given[i], max(1, budget * portions[i] // mass), surplus)
            given[i] = given[i] + extra
            surplus = surplus - extra
    return np.array([limit] + given)


def ragged(own_key, number_of, total, reach, slope):
    if number_of == 2:
        one = jax.random.randint(own_key, (), max(1, total - reach), min(reach, total - 1) + 1)
        return jnp.stack([one, total - one])
    lengths = jnp.asarray(length_profile(number_of, total, reach, slope), jnp.int32)
    twos = (number_of - 1) // 2
    source_of, sink = lengths[1:1 + 2 * twos:2], lengths[2:2 + 2 * twos:2]
    margin = jnp.minimum(source_of - 1, reach - sink)
    moved = jax.random.randint(jax.random.fold_in(own_key, 1), (twos,), 0, 1 << 20) % (margin + 1)
    lengths = lengths.at[1:1 + 2 * twos:2].set(source_of - moved).at[2:2 + 2 * twos:2].set(sink + moved)
    return lengths[jax.random.permutation(jax.random.fold_in(own_key, 2), number_of)]


def scatter_about(rng, dims, deviation, most, held_as=jnp.bfloat16):
    return jnp.clip(deviation * jax.random.normal(rng, dims, jnp.float32), -most, most).astype(held_as)


def setup_inputs(seed: int = 0, part: int = 0) -> dict:
    arg_keys = jax.random.split(jax.random.key(seed), 5)
    part_keys = jax.random.split(jax.random.fold_in(arg_keys[4], part), 5)
    frames = draw_frames(jax.random.fold_in(jax.random.fold_in(arg_keys[4], part), 71), part)
    episode_lengths = ragged(part_keys[1], EPISODES, SEQ, EPI_MAX, 2).astype(jnp.int32)
    w_qkv = draw_w_qkv(jax.random.fold_in(arg_keys[4], 71), part)
    w_out = scatter_about(arg_keys[3], (D, D), D ** -0.5, 0.25)
    return {"frames": frames, "episode_lengths": episode_lengths, "w_qkv": w_qkv, "w_out": w_out}


def normalize(rows):
    wide = rows.astype(jnp.float32)
    factor = lax.rsqrt(lax.optimization_barrier(jnp.mean(wide * wide, axis=-1, keepdims=True)) + 1e-06)
    return (wide * factor).astype(jnp.bfloat16)

def episode_start(positions, episode_lengths):
    ends = jnp.cumsum(episode_lengths).astype(jnp.int32)
    passed = (ends[None, :] <= positions[:, None]).astype(jnp.int32)
    return lax.optimization_barrier(jnp.sum(passed * episode_lengths[None, :], axis=1)).astype(jnp.int32)

def attend(queries, keys, values, query_pos, key_pos, starts):
    allowed = (key_pos[None, :] <= query_pos[:, None]) & (key_pos[None, :] >= starts[:, None])
    outputs = []
    for head in range(HEADS):
        low = head * HEAD_DIM
        high = low + HEAD_DIM
        scores = lax.dot_general(queries[:, low:high], keys[:, low:high], (((1,), (1,)), ((), ())), preferred_element_type=jnp.float32)
        scores = scores * HEAD_DIM ** (-0.5)
        scores = jnp.where(allowed, scores, -jnp.inf)
        peak = lax.optimization_barrier(jnp.max(scores, axis=1, keepdims=True))
        weights = jnp.exp(scores - peak)
        totals = lax.optimization_barrier(jnp.sum(weights, axis=1, keepdims=True))
        mixed = jnp.dot(weights.astype(jnp.bfloat16), values[:, low:high], preferred_element_type=jnp.float32) / totals
        outputs.append(mixed)
    return jnp.concatenate(outputs, axis=1).astype(jnp.bfloat16)

def reference(frames, episode_lengths, w_qkv, w_out):
    lower = frames[:, 0]
    upper = frames[::-1, 1]
    tokens = jnp.concatenate([lower, upper], axis=0).reshape(SEQ, D)
    normed = normalize(tokens)
    projected = jnp.dot(normed, w_qkv, preferred_element_type=jnp.float32).astype(jnp.bfloat16)
    queries = projected[:, :D]
    padding = jnp.zeros((WIN * CH, D), jnp.bfloat16)
    keys = jnp.concatenate([padding, projected[:, D:2 * D]], axis=0)
    values = jnp.concatenate([padding, projected[:, 2 * D:]], axis=0)
    positions = jnp.arange(SEQ, dtype=jnp.int32)
    starts = episode_start(positions, episode_lengths)

    def block(index):
        first = (index * CH).astype(jnp.int32)
        query_rows = lax.dynamic_slice_in_dim(queries, first, CH, 0)
        key_rows = lax.dynamic_slice_in_dim(keys, first, (WIN + 1) * CH, 0)
        value_rows = lax.dynamic_slice_in_dim(values, first, (WIN + 1) * CH, 0)
        block_starts = lax.dynamic_slice_in_dim(starts, first, CH, 0)
        query_pos = first + jnp.arange(CH, dtype=jnp.int32)
        key_pos = first - WIN * CH + jnp.arange((WIN + 1) * CH, dtype=jnp.int32)
        mixed = attend(query_rows, key_rows, value_rows, query_pos, key_pos, block_starts)
        return jnp.dot(mixed, w_out, preferred_element_type=jnp.float32).astype(jnp.bfloat16)
    result = lax.map(block, jnp.arange(2 * N_CTX, dtype=jnp.int32))
    return jnp.stack([result[:N_CTX], result[N_CTX:][::-1]], axis=1)
```

```python
import functools

import jax
import jax.numpy as jnp
from jax import lax
from jax.experimental import pallas as pl
from jax.experimental.pallas import tpu as pltpu
from jax.sharding import PartitionSpec as P


HEADS = 4
HEAD_DIM = 128
LANES = 128
WIDE = HEAD_DIM + LANES
SCALE2 = HEAD_DIM ** (-0.5) * 1.4426950408889634
VMEM = pl.BlockSpec(memory_space=pltpu.VMEM)
SMEM = pl.BlockSpec(memory_space=pltpu.SMEM)
F32 = jnp.float32
BF16 = jnp.bfloat16


def normalize(rows):
    wide = rows.astype(F32)
    factor = lax.rsqrt(jnp.mean(wide * wide, axis=-1, keepdims=True) + 1e-06)
    return (wide * factor).astype(BF16)


def matmul(left, right):
    return jnp.dot(left, right, preferred_element_type=F32)


def where_am_i():
    place = lax.axis_index("ctx")
    return place, lax.rem(place // 2, 2), lax.rem(place, 2)


def block_first(half, place, count, group):
    return jnp.where(half == 0, place, 2 * count - 1 - place) * group


def start_of(position, lengths_ref, zero):
    def step(e, carry):
        end, start = carry
        end = end + lengths_ref[e]
        return end, jnp.where(end <= position, end, start)

    return lax.fori_loop(0, lengths_ref.shape[0], step, (jnp.int32(0), zero))[1]


def fill_starts(starts_ref, lengths_ref, first):
    for low in range(0, starts_ref.shape[0], LANES):
        position = first + low + lax.broadcasted_iota(jnp.int32, (8, LANES), 1)
        start = start_of(position, lengths_ref, jnp.zeros_like(position))
        wide = jnp.concatenate([start] * (LANES // 8), axis=0)
        starts_ref[low : low + LANES, :] = jnp.transpose(wide)


def across(column, width):
    return jnp.concatenate([column] * (width // LANES), axis=1)


def attend_tile(q_ref, starts_ref, keys_ref, values_ref, old, new, row, rows, low, size, key_first, diag):
    rs = pl.ds(row, rows)
    key = key_first + low + lax.broadcasted_iota(jnp.int32, (rows, size), 1)
    allowed = key >= across(starts_ref[rs, :], size)
    if diag:
        query = key_first + row + lax.broadcasted_iota(jnp.int32, (rows, size), 0)
        allowed = allowed & (key <= query)
    for head in range(HEADS):
        hs = pl.ds(head * HEAD_DIM, HEAD_DIM)
        ws = pl.ds(head * WIDE, WIDE)
        scores = lax.dot_general(
            q_ref[rs, hs],
            keys_ref[pl.ds(low, size), hs],
            (((1,), (1,)), ((), ())),
            preferred_element_type=F32,
        )
        scores = jnp.where(allowed, scores, -jnp.inf)
        peak = jnp.broadcast_to(jnp.max(scores, axis=1, keepdims=True), (rows, LANES))
        if old is not None:
            before = old[1][rs, hs]
            peak = jnp.maximum(before, peak)
        weights = jnp.exp2((scores - across(peak, size)) * SCALE2)
        mixed = matmul(weights.astype(BF16), values_ref[pl.ds(low, size), ws])
        if old is not None:
            fade = jnp.exp2((before - peak) * SCALE2)
            mixed = mixed + across(fade, WIDE) * old[0][rs, ws]
        new[1][rs, hs] = peak
        new[0][rs, ws] = mixed


def project_pair(normed, w_ref, keys_ref, values_ref):
    rows, width = normed.shape
    keys_ref[...] = matmul(normed, w_ref[:, width : 2 * width]).astype(BF16)
    values = matmul(normed, w_ref[:, 2 * width :]).astype(BF16)
    for head in range(HEADS):
        values_ref[:, head * WIDE : head * WIDE + HEAD_DIM] = values[
            :, head * HEAD_DIM : (head + 1) * HEAD_DIM
        ]
        values_ref[:, head * WIDE + HEAD_DIM : (head + 1) * WIDE] = jnp.ones((rows, LANES), BF16)


def attend_block(q_ref, starts_ref, keys_ref, values_ref, old, new, first, behind, lengths_ref):
    group = keys_ref.shape[0]
    rows = group // 2
    key_first = first - behind * group
    for row in range(0, group, rows):
        low = row if behind == 2 else 0
        reach = start_of(first + row, lengths_ref, jnp.int32(0))

        @pl.when(reach < key_first + group)
        def _():
            attend_tile(
                q_ref, starts_ref, keys_ref, values_ref, old, new,
                row, rows, low, group - low, key_first, False,
            )

        if old is not new:
            @pl.when(reach >= key_first + group)
            def _():
                for o, n in zip(old, new):
                    n[pl.ds(row, rows), :] = o[pl.ds(row, rows), :]


def finish(acc_ref, w_out_ref):
    parts = []
    for head in range(HEADS):
        low = head * WIDE
        mixed = acc_ref[:, low : low + HEAD_DIM] / acc_ref[:, low + HEAD_DIM : low + WIDE]
        parts.append(mixed.astype(BF16))
    return matmul(jnp.concatenate(parts, axis=1), w_out_ref[...]).astype(BF16)


def prepare_kernel(frames_ref, straight_ref, cross_a_ref, cross_b_ref):
    side = lax.rem(lax.axis_index("ctx") // 2, 2)
    straight_ref[...] = normalize(frames_ref[0, side])
    rows = cross_a_ref.shape[0]
    cross_a_ref[...] = normalize(frames_ref[0, 1 - side, :rows])
    cross_b_ref[...] = normalize(frames_ref[0, 1 - side, rows:])


def own_kernel(count, late, lengths_ref, *refs):
    parts, (partner_ref, w_ref, q_ref, acc_ref, m_ref, starts_ref, keys_ref, values_ref, block_ref) = (
        refs[:-9], refs[-9:],
    )
    place, side, core = where_am_i()
    half = side if late else 1 - side
    group, width = block_ref.shape
    first = block_first(half, place, count, group)
    fill_starts(starts_ref, lengths_ref, first)
    low = 0
    for part in parts:
        block_ref[low : low + part.shape[0], :] = part[...]
        low += part.shape[0]
    normed = block_ref[...]
    q_ref[...] = matmul(normed, w_ref[:, :width]).astype(BF16)
    project_pair(normed, w_ref, keys_ref, values_ref)
    state = (acc_ref, m_ref)
    rows = group // 2
    for row in range(0, group, rows):
        attend_tile(
            q_ref, starts_ref, keys_ref, values_ref, None, state, row, rows, 0, row + rows, first, True
        )

    @pl.when(half == 1 - core)
    def _():
        project_pair(normalize(partner_ref[0, half]), w_ref, keys_ref, values_ref)
        attend_block(
            q_ref, starts_ref, keys_ref, values_ref, state, state, first, 1, lengths_ref
        )


def far_kernel(count, late, lengths_ref, *refs):
    parts, (partner_ref, w_ref, q_ref, acc_in, m_in, starts_ref, acc_ref, m_ref, keys_ref, values_ref, block_ref) = (
        refs[:-11], refs[-11:],
    )
    place, side, _ = where_am_i()
    half = side if late else 1 - side
    group, _ = block_ref.shape
    first = block_first(half, place, count, group)
    low = 0
    for part in parts:
        block_ref[low : low + part.shape[0], :] = part[...]
        low += part.shape[0]
    if late:
        @pl.when(place // 2 == count // 2 - 1)
        def _():
            block_ref[...] = normalize(partner_ref[0, 0])

    project_pair(block_ref[...], w_ref, keys_ref, values_ref)
    attend_block(
        q_ref, starts_ref, keys_ref, values_ref,
        (acc_in, m_in), (acc_ref, m_ref), first, 2, lengths_ref,
    )


def near_kernel(count, late, lengths_ref, *refs):
    n = 2 if late else 1
    parts = refs[:n]
    own = refs[n : n + 2]
    w_ref, w_out_ref, q_ref, acc_in, m_in, starts_ref = refs[n + 2 : n + 8]
    out_ref, acc_ref, m_ref, keys_ref, values_ref, block_ref = refs[-6:]
    place, side, core = where_am_i()
    half = side if late else 1 - side
    group, _ = block_ref.shape
    first = block_first(half, place, count, group)
    state = (acc_ref, m_ref)

    @pl.when(half == core)
    def _():
        low = 0
        for part in parts:
            block_ref[low : low + part.shape[0], :] = part[...]
            low += part.shape[0]
        if late:
            @pl.when(place == count - 1)
            def _():
                low = 0
                for part in own:
                    block_ref[low : low + part.shape[0], :] = part[...]
                    low += part.shape[0]

        project_pair(block_ref[...], w_ref, keys_ref, values_ref)
        attend_block(
            q_ref, starts_ref, keys_ref, values_ref,
            (acc_in, m_in), state, first, 1, lengths_ref,
        )

    @pl.when(half != core)
    def _():
        acc_ref[...] = acc_in[...]

    out = finish(acc_ref, w_out_ref)
    if late:
        out_ref[0, half] = out
        out_ref[0, 1 - half] = refs[n + 8][...]
    else:
        out_ref[...] = out


def params(mib):
    return pltpu.CompilerParams(vmem_limit_bytes=mib * 1024 * 1024)


def local(frames, episode_lengths, w_qkv, w_out):
    width = w_out.shape[0]
    group = frames.shape[2]
    count = lax.axis_size("ctx")
    chips = count // 2
    pair = [(i, i ^ 1) for i in range(count)]

    def route(links):
        return [(2 * a + c, 2 * b + c) for a, b in links for c in range(2)]

    even = [(c, c + 1) for c in range(0, chips - 1, 2)]
    odd = [(c, c + 1) for c in range(1, chips - 1, 2)]
    swap_x = route(even + [(b, a) for a, b in even])
    swap_d = route(odd + [(b, a) for a, b in odd])
    relay_out = route([(a, b + 1) for a, b in odd] + [(b, a - 1) for a, b in odd])
    relay_in = route([(b + 1, b) for a, b in odd] + [(a - 1, a) for a, b in odd])

    def send(block, links):
        return lax.ppermute(block, "ctx", links)

    def shape(*dims, dtype=BF16):
        return jax.ShapeDtypeStruct(dims, dtype)

    block = shape(group, width)
    part = shape(group // 2, width)
    q_type = shape(group, width)
    acc_type = shape(group, HEADS * WIDE, dtype=F32)
    m_type = shape(group, width, dtype=F32)
    starts_type = shape(group, LANES, dtype=jnp.int32)
    scratch = [
        pltpu.VMEM((group, width), BF16),
        pltpu.VMEM((group, HEADS * WIDE), BF16),
        pltpu.VMEM((group, width), BF16),
    ]

    def call(kernel, late, outs, operands, more=(), flops=2):
        return pl.pallas_call(
            functools.partial(kernel, count, late),
            out_shape=outs,
            in_specs=[SMEM] + [VMEM] * (len(operands) - 1),
            out_specs=jax.tree.map(lambda _: VMEM, outs),
            scratch_shapes=list(more) + scratch,
            compiler_params=params(12),
            cost_estimate=pl.CostEstimate(
                flops=flops * 10**8, bytes_accessed=10**6, transcendentals=0
            ),
        )(*operands)

    partner = send(frames, pair)
    straight, cross_a, cross_b = pl.pallas_call(
        prepare_kernel,
        out_shape=(block, part, part),
        in_specs=[VMEM],
        out_specs=(VMEM,) * 3,
        compiler_params=params(4),
    )(frames)
    hop_in = send(cross_a, relay_out)
    x_in = send(straight, swap_x)
    d_in = send(cross_b, swap_d)
    states = (q_type, acc_type, m_type, starts_type)
    q_x, acc_x, m_x, starts_x = call(
        own_kernel, False, states, (episode_lengths, cross_a, cross_b, partner, w_qkv)
    )
    hop_in, q_x = lax.optimization_barrier((hop_in, q_x))
    r_in = send(hop_in, relay_in)
    q_d, acc_d, m_d, starts_d = call(
        own_kernel, True, states, (episode_lengths, straight, partner, w_qkv)
    )
    x_in, q_d = lax.optimization_barrier((x_in, q_d))
    near_x = send(x_in, pair)
    acc_x, m_x = call(
        far_kernel, False, (acc_type, m_type),
        (episode_lengths, x_in, partner, w_qkv, q_x, acc_x, m_x, starts_x),
    )
    state_scratch = (pltpu.VMEM(acc_type.shape, F32), pltpu.VMEM(m_type.shape, F32))
    out_x = call(
        near_kernel, False, block,
        (episode_lengths, near_x, cross_a, cross_b, w_qkv, w_out, q_x, acc_x, m_x, starts_x),
        state_scratch,
    )
    r_in, d_in, out_x = lax.optimization_barrier((r_in, d_in, out_x))
    near_b = send(d_in, pair)
    near_a = send(r_in, pair)
    acc_d, m_d = call(
        far_kernel, True, (acc_type, m_type),
        (episode_lengths, r_in, d_in, partner, w_qkv, q_d, acc_d, m_d, starts_d),
    )
    return call(
        near_kernel, True, jax.ShapeDtypeStruct(frames.shape, BF16),
        (episode_lengths, near_a, near_b, cross_a, cross_b, w_qkv, w_out, q_d, acc_d, m_d, starts_d, out_x),
        state_scratch,
    )


def solution(mesh):
    in_specs = (P(("dp", "ctx"), None, None, None), P("dp"), P(), P())
    out_specs = P(("dp", "ctx"), None, None, None)
    return jax.shard_map(local, mesh=mesh, in_specs=in_specs, out_specs=out_specs, check_vma=False)
```

```python
import functools

import jax
import jax.numpy as jnp
from jax import lax
from jax.experimental import pallas as pl
from jax.experimental.pallas import tpu as pltpu
from jax.sharding import PartitionSpec as P


HEADS = 4
HEAD_DIM = 128
LANES = 128
WIDE = HEAD_DIM + LANES
SCALE2 = HEAD_DIM ** (-0.5) * 1.4426950408889634
APART = -1e30
VMEM = pl.BlockSpec(memory_space=pltpu.VMEM)
SMEM = pl.BlockSpec(memory_space=pltpu.SMEM)
HBM = pl.BlockSpec(memory_space=pltpu.HBM)
F32 = jnp.float32
BF16 = jnp.bfloat16


def normalize(rows):
    wide = rows.astype(F32)
    factor = lax.rsqrt(jnp.mean(wide * wide, axis=-1, keepdims=True) + 1e-06)
    return (wide * factor).astype(BF16)


def matmul(left, right):
    return jnp.dot(left, right, preferred_element_type=F32)


def where_am_i():
    place = lax.axis_index("ctx")
    return place, lax.rem(place // 2, 2), lax.rem(place, 2)


def block_first(half, place, count, group):
    return jnp.where(half == 0, place, 2 * count - 1 - place) * group


def beside(left, right):
    return jnp.concatenate([left, right], axis=1)


def across(column, width):
    return jnp.concatenate([column] * (width // LANES), axis=1)


def inside(bounds_ref, first, rows):
    position = first + lax.broadcasted_iota(jnp.int32, (rows, LANES), 0)
    return (position >= bounds_ref[0:1, :]) & (position < bounds_ref[1:2, :])


def query_marks(bounds_ref, first, rows):
    return jnp.where(inside(bounds_ref, first, rows), 1.0, 0.0).astype(BF16)


def key_marks(bounds_ref, first, rows):
    return jnp.where(inside(bounds_ref, first, rows), 0.0, APART).astype(BF16)


def attend(q_ref, marks, pair, old, tiles):
    keys_ref, values_ref, key_marks_ref = pair
    rows = marks.shape[0]
    out = []
    for head in range(HEADS):
        hs = pl.ds(head * HEAD_DIM, HEAD_DIM)
        ws = pl.ds(head * WIDE, WIDE)
        query = beside(q_ref[:, hs], marks)
        scores, peaks = [], []
        for low, size, top, bottom, causal in tiles:
            cs = pl.ds(low, size)
            tile = lax.dot_general(
                query[top:bottom],
                beside(keys_ref[cs, hs], key_marks_ref[cs, :]),
                (((1,), (1,)), ((), ())),
                preferred_element_type=F32,
            )
            if causal:
                here = lax.broadcasted_iota(jnp.int32, (size, size), 0)
                there = lax.broadcasted_iota(jnp.int32, (size, size), 1)
                edge = jnp.where(there <= here, tile[:size], APART)
                tile = jnp.concatenate([edge, tile[size:]], axis=0) if bottom - top > size else edge
            scores.append(tile)
            peak = jnp.max(tile, axis=1, keepdims=True)
            peaks.append(jnp.broadcast_to(peak, (bottom - top, LANES)))
        peak = spread(jnp.maximum, [(p, t[2], t[3]) for p, t in zip(peaks, tiles)], rows)
        if old is not None:
            before = old[1][:, hs]
            peak = jnp.maximum(before, peak)
        mixes = []
        for tile, (low, size, top, bottom, _) in zip(scores, tiles):
            weights = jnp.exp2(tile - across(peak[top:bottom], size)).astype(BF16)
            ones = jnp.ones((size, LANES), BF16)
            mix = matmul(weights, beside(values_ref[pl.ds(low, size), hs], ones))
            mixes.append((mix, top, bottom))
        mixed = spread(jnp.add, mixes, rows)
        if old is not None:
            mixed = mixed + across(jnp.exp2(before - peak), WIDE) * old[0][:, ws]
        out.append((mixed, peak))
    return out


def spread(combine, items, rows):
    whole = [item for item, top, bottom in items if bottom - top == rows]
    total = whole[0]
    for item, top, bottom in items:
        if bottom - top == rows:
            continue
        pieces = [total[:top]] if top else []
        pieces.append(combine(total[top:bottom], item))
        if bottom < rows:
            pieces.append(total[bottom:])
        total = jnp.concatenate(pieces, axis=0)
    return total


def keep(out, new):
    for head, (mixed, peak) in enumerate(out):
        new[0][:, head * WIDE : (head + 1) * WIDE] = mixed
        new[1][:, head * HEAD_DIM : (head + 1) * HEAD_DIM] = peak


def project_pair(normed, first, bounds_ref, w_ref, pair):
    rows, width = normed.shape
    keys_ref, values_ref, key_marks_ref = pair
    keys_ref[...] = matmul(normed, w_ref[:, width : 2 * width]).astype(BF16)
    values_ref[...] = matmul(normed, w_ref[:, 2 * width :]).astype(BF16)
    key_marks_ref[...] = key_marks(bounds_ref, first, rows)


def gather(parts, block_ref):
    low = 0
    for part in parts:
        block_ref[low : low + part.shape[0], :] = part[...]
        low += part.shape[0]


def prepare_kernel(frames_ref, lengths_ref, straight_ref, cross_a_ref, cross_b_ref, bounds_ref):
    _, side, _ = where_am_i()
    straight_ref[...] = normalize(frames_ref[0, side])
    rows = cross_a_ref.shape[0]
    cross_a_ref[...] = normalize(frames_ref[0, 1 - side, :rows])
    cross_b_ref[...] = normalize(frames_ref[0, 1 - side, rows:])
    lane = lax.broadcasted_iota(jnp.int32, (8, LANES), 1)
    row = lax.broadcasted_iota(jnp.int32, (8, LANES), 0)

    def step(e, carry):
        begin, bounds = carry
        end = begin + lengths_ref[e]
        return end, jnp.where(lane == e, jnp.where(row == 0, begin, end), bounds)

    bounds_ref[...] = lax.fori_loop(
        0, lengths_ref.shape[0], step, (jnp.int32(0), jnp.zeros((8, LANES), jnp.int32)),
        unroll=True,
    )[1]


def own_block(normed, first, bounds_ref, w_ref, q_ref, state, pair):
    group, width = normed.shape
    rows = group // 2
    q_ref[...] = (matmul(normed, w_ref[:, :width]) * SCALE2).astype(BF16)
    project_pair(normed, first, bounds_ref, w_ref, pair)
    marks = query_marks(bounds_ref, first, group)
    tiles = ((0, rows, 0, group, True), (rows, rows, rows, group, True))
    keep(attend(q_ref, marks, pair, None, tiles), state)


def own_x_kernel(
    count, bounds_ref, cross_a_ref, cross_b_ref, w_ref, q_ref, acc_ref, m_ref, block_ref, *pair
):
    place, side, _ = where_am_i()
    half = 1 - side
    first = block_first(half, place, count, block_ref.shape[0])
    gather((cross_a_ref, cross_b_ref), block_ref)
    own_block(block_ref[...], first, bounds_ref, w_ref, q_ref, (acc_ref, m_ref), pair)


def own_d_kernel(
    count, bounds_ref, straight_ref, partner_ref, w_ref, q_x_ref, acc_in, m_in,
    q_ref, acc_ref, m_ref, acc_x_ref, m_x_ref, block_ref, *pair
):
    place, side, core = where_am_i()
    group = straight_ref.shape[0]
    first = block_first(side, place, count, group)
    state = (acc_ref, m_ref)
    own_block(straight_ref[...], first, bounds_ref, w_ref, q_ref, state, pair)
    half = 1 - core
    first = block_first(half, place, count, group)
    project_pair(normalize(partner_ref[0, half]), first - group, bounds_ref, w_ref, pair)
    marks = query_marks(bounds_ref, first, group)
    tiles = ((0, group, 0, group, False),)

    @pl.when(half == side)
    def _():
        keep(attend(q_ref, marks, pair, state, tiles), state)
        acc_x_ref[...] = acc_in[...]
        m_x_ref[...] = m_in[...]

    @pl.when(half != side)
    def _():
        keep(attend(q_x_ref, marks, pair, (acc_in, m_in), tiles), (acc_x_ref, m_x_ref))


def far_kernel(
    count, late, bounds_ref, far_ref, partner_ref, w_ref, q_ref, acc_in, m_in,
    acc_ref, m_ref, block_ref, *pair
):
    place, side, _ = where_am_i()
    half = side if late else 1 - side
    group, _ = far_ref.shape
    first = block_first(half, place, count, group)
    rows = group // 2
    block_ref[...] = far_ref[...]
    if late:
        @pl.when(place // 2 == count // 2 - 1)
        def _():
            block_ref[...] = normalize(partner_ref[0, 0])

    project_pair(block_ref[...], first - 2 * group, bounds_ref, w_ref, pair)
    marks = query_marks(bounds_ref, first, group)
    tiles = ((rows, rows, 0, group, False), (0, rows, 0, rows, False))
    keep(attend(q_ref, marks, pair, (acc_in, m_in), tiles), (acc_ref, m_ref))


def near_kernel(count, late, bounds_ref, near_ref, cross_a_ref, cross_b_ref, *refs):
    w_ref, w_out_ref, q_ref, acc_in, m_in = refs[:5]
    out_ref, stage_ref, sems, block_ref = refs[-7:-3]
    pair = refs[-3:]
    place, side, core = where_am_i()
    half = side if late else 1 - side
    group, _ = block_ref.shape
    first = block_first(half, place, count, group)
    rows = group // 2

    def emit(wide):
        for row in range(0, group, rows):
            rs = slice(row, row + rows)
            mixed = [(m[rs, :HEAD_DIM] / m[rs, HEAD_DIM:]).astype(BF16) for m in wide]
            out = matmul(jnp.concatenate(mixed, axis=1), w_out_ref[...])
            stage_ref[rs, :] = out.astype(BF16)
            copy_out(row).start()

    def copy_out(row):
        rs = pl.ds(row, rows)
        return pltpu.make_async_copy(
            stage_ref.at[rs], out_ref.at[0, half, rs], sems.at[row // rows]
        )

    @pl.when(half == core)
    def _():
        block_ref[...] = near_ref[...]
        if late:
            @pl.when(place == count - 1)
            def _():
                gather((cross_a_ref, cross_b_ref), block_ref)

        project_pair(block_ref[...], first - group, bounds_ref, w_ref, pair)
        marks = query_marks(bounds_ref, first, group)
        out = attend(q_ref, marks, pair, (acc_in, m_in), ((0, group, 0, group, False),))
        emit([mixed for mixed, _ in out])

    @pl.when(half != core)
    def _():
        emit([acc_in[:, h * WIDE : (h + 1) * WIDE] for h in range(HEADS)])

    for row in range(0, group, rows):
        copy_out(row).wait()


def params(mib):
    return pltpu.CompilerParams(vmem_limit_bytes=mib * 1024 * 1024)


def local(frames, episode_lengths, w_qkv, w_out):
    width = w_out.shape[0]
    group = frames.shape[2]
    count = lax.axis_size("ctx")
    chips = count // 2
    pair = [(i, i ^ 1) for i in range(count)]

    def route(links):
        return [(2 * a + c, 2 * b + c) for a, b in links for c in range(2)]

    even = [(c, c + 1) for c in range(0, chips - 1, 2)]
    odd = [(c, c + 1) for c in range(1, chips - 1, 2)]
    swap_x = route(even + [(b, a) for a, b in even])
    swap_d = route(odd + [(b, a) for a, b in odd])
    relay_out = route([(a, b + 1) for a, b in odd] + [(b, a - 1) for a, b in odd])
    relay_in = route([(b + 1, b) for a, b in odd] + [(a - 1, a) for a, b in odd])

    def send(block, links):
        return lax.ppermute(block, "ctx", links)

    def shape(*dims, dtype=BF16):
        return jax.ShapeDtypeStruct(dims, dtype)

    block = shape(group, width)
    part = shape(group // 2, width)
    acc_type = shape(group, HEADS * WIDE, dtype=F32)
    m_type = shape(group, width, dtype=F32)
    scratch = [pltpu.VMEM((group, width), BF16)] * 3 + [pltpu.VMEM((group, LANES), BF16)]

    def call(kernel, outs, operands, aliased=None):
        specs = [VMEM] * len(operands)
        options = dict(out_specs=(VMEM,) * len(outs), scratch_shapes=scratch)
        if aliased is not None:
            options["out_specs"] = (HBM,)
            options["scratch_shapes"] = [
                pltpu.VMEM((group, width), BF16), pltpu.SemaphoreType.DMA((2,)),
            ] + scratch
        if aliased:
            specs.append(HBM)
            options["input_output_aliases"] = {len(operands): 0}
            operands = operands + aliased
        return pl.pallas_call(
            kernel,
            out_shape=outs,
            in_specs=specs,
            compiler_params=params(14),
            cost_estimate=pl.CostEstimate(flops=10**8, bytes_accessed=10**6, transcendentals=0),
            **options,
        )(*operands)

    partner = send(frames, pair)
    straight, cross_a, cross_b, bounds = pl.pallas_call(
        prepare_kernel,
        out_shape=(block, part, part, shape(8, LANES, dtype=jnp.int32)),
        in_specs=[VMEM, SMEM],
        out_specs=(VMEM,) * 4,
        compiler_params=params(4),
        cost_estimate=pl.CostEstimate(flops=10**10, bytes_accessed=10**6, transcendentals=0),
    )(frames, episode_lengths)
    w = w_qkv
    hop_in = send(cross_a, relay_out)
    x_in = send(straight, swap_x)
    d_in = send(cross_b, swap_d)
    bind = functools.partial
    state = (acc_type, m_type)
    q_x, acc_x, m_x = call(
        bind(own_x_kernel, count), (block,) + state, (bounds, cross_a, cross_b, w)
    )
    hop_in, q_x = lax.optimization_barrier((hop_in, q_x))
    r_in = send(hop_in, relay_in)
    q_d, acc_d, m_d, acc_x, m_x = call(
        bind(own_d_kernel, count), (block,) + state + state,
        (bounds, straight, partner, w, q_x, acc_x, m_x),
    )
    x_in, q_d = lax.optimization_barrier((x_in, q_d))
    near_x = send(x_in, pair)
    acc_x, m_x = call(
        bind(far_kernel, count, False), state,
        (bounds, x_in, partner, w, q_x, acc_x, m_x),
    )
    whole = (jax.ShapeDtypeStruct(frames.shape, BF16),)
    (out,) = call(
        bind(near_kernel, count, False), whole,
        (bounds, near_x, cross_a, cross_b, w, w_out, q_x, acc_x, m_x), (),
    )
    r_in, d_in, out = lax.optimization_barrier((r_in, d_in, out))
    d_block = jnp.concatenate([r_in, d_in], axis=0)
    near_d = send(d_block, pair)
    acc_d, m_d = call(
        bind(far_kernel, count, True), state,
        (bounds, d_block, partner, w, q_d, acc_d, m_d),
    )
    (out,) = call(
        bind(near_kernel, count, True), whole,
        (bounds, near_d, cross_a, cross_b, w, w_out, q_d, acc_d, m_d), (out,),
    )
    return out


def solution(mesh):
    in_specs = (P(("dp", "ctx"), None, None, None), P("dp"), P(), P())
    out_specs = P(("dp", "ctx"), None, None, None)
    return jax.shard_map(local, mesh=mesh, in_specs=in_specs, out_specs=out_specs, check_vma=False)
```

```python
import functools

import jax
import jax.numpy as jnp
from jax import lax
from jax.experimental import pallas as pl
from jax.experimental.pallas import tpu as pltpu
from jax.sharding import PartitionSpec as P


HEADS = 4
HEAD_DIM = 128
LANES = 128
WIDE = HEAD_DIM + LANES
SCALE2 = HEAD_DIM ** (-0.5) * 1.4426950408889634
APART = -1e30
VMEM = pl.BlockSpec(memory_space=pltpu.VMEM)
HBM = pl.BlockSpec(memory_space=pltpu.HBM)
F32 = jnp.float32
BF16 = jnp.bfloat16


def normalize(rows):
    wide = rows.astype(F32)
    factor = lax.rsqrt(jnp.mean(wide * wide, axis=-1, keepdims=True) + 1e-06)
    return (wide * factor).astype(BF16)


def matmul(left, right):
    return jnp.dot(left, right, preferred_element_type=F32)


def where_am_i():
    place = lax.axis_index("ctx")
    return place, lax.rem(place // 2, 2), lax.rem(place, 2)


def block_first(half, place, count, group):
    return jnp.where(half == 0, place, 2 * count - 1 - place) * group


def beside(left, right):
    return jnp.concatenate([left, right], axis=1)


def across(column, width):
    return jnp.concatenate([column] * (width // LANES), axis=1)


def inside(bounds, first, rows):
    position = first + lax.broadcasted_iota(jnp.int32, (rows, LANES), 0)
    return (position >= bounds[0:1, :]) & (position < bounds[1:2, :])


def fill_starts(starts_ref, bounds, first):
    rows = starts_ref.shape[0]
    chosen = jnp.where(inside(bounds, first, rows), bounds[0:1, :], 0)
    start = jnp.sum(chosen.astype(F32), axis=1, keepdims=True).astype(jnp.int32)
    starts_ref[...] = jnp.broadcast_to(start, starts_ref.shape)


def attend(q_ref, starts_ref, kv_ref, key_first, old, tiles):
    rows, width = q_ref.shape
    out = []
    for head in range(HEADS):
        hs = pl.ds(head * HEAD_DIM, HEAD_DIM)
        vs = pl.ds(width + head * HEAD_DIM, HEAD_DIM)
        ws = pl.ds(head * WIDE, WIDE)
        scores, peaks = [], []
        for low, size, top, bottom, causal in tiles:
            tile = lax.dot_general(
                q_ref[pl.ds(top, bottom - top), hs],
                kv_ref[pl.ds(low, size), hs],
                (((1,), (1,)), ((), ())),
                preferred_element_type=F32,
            )
            reach = starts_ref[pl.ds(top, bottom - top), :] - (key_first + low)
            there = lax.broadcasted_iota(jnp.int32, tile.shape, 1)
            allowed = there >= across(reach, size)
            if causal:
                here = lax.broadcasted_iota(jnp.int32, tile.shape, 0)
                allowed = allowed & (there <= here)
            tile = jnp.where(allowed, tile, APART)
            scores.append(tile)
            peak = jnp.max(tile, axis=1, keepdims=True)
            peaks.append(jnp.broadcast_to(peak, (bottom - top, LANES)))
        peak = spread(jnp.maximum, [(p, t[2], t[3]) for p, t in zip(peaks, tiles)], rows)
        if old is not None:
            before = old[1][:, hs]
            peak = jnp.maximum(before, peak)
        mixes = []
        for tile, (low, size, top, bottom, _) in zip(scores, tiles):
            weights = jnp.exp2(tile - across(peak[top:bottom], size)).astype(BF16)
            ones = jnp.ones((size, LANES), BF16)
            mix = matmul(weights, beside(kv_ref[pl.ds(low, size), vs], ones))
            mixes.append((mix, top, bottom))
        mixed = spread(jnp.add, mixes, rows)
        if old is not None:
            mixed = mixed + across(jnp.exp2(before - peak), WIDE) * old[0][:, ws]
        out.append((mixed, peak))
    return out


def spread(combine, items, rows):
    whole = [item for item, top, bottom in items if bottom - top == rows]
    total = whole[0]
    for item, top, bottom in items:
        if bottom - top == rows:
            continue
        pieces = [total[:top]] if top else []
        pieces.append(combine(total[top:bottom], item))
        if bottom < rows:
            pieces.append(total[bottom:])
        total = jnp.concatenate(pieces, axis=0)
    return total


def keep(out, new):
    for head, (mixed, peak) in enumerate(out):
        new[0][:, head * WIDE : (head + 1) * WIDE] = mixed
        new[1][:, head * HEAD_DIM : (head + 1) * HEAD_DIM] = peak


def diagonal(group):
    rows = group // 2
    return ((0, rows, 0, group, True), (rows, rows, rows, group, True))


def full(group):
    return ((0, group, 0, group, False),)


def beyond(group):
    rows = group // 2
    return ((rows, rows, 0, group, False), (0, rows, 0, rows, False))


def gather(parts, block_ref):
    low = 0
    for part in parts:
        block_ref[low : low + part.shape[0], :] = part[...]
        low += part.shape[0]


def prepare_kernel(frames_ref, straight_ref, cross_a_ref, cross_b_ref):
    _, side, _ = where_am_i()
    straight_ref[...] = normalize(frames_ref[0, side])
    rows = cross_a_ref.shape[0]
    cross_a_ref[...] = normalize(frames_ref[0, 1 - side, :rows])
    cross_b_ref[...] = normalize(frames_ref[0, 1 - side, rows:])


def bounds_of(lengths_ref):
    lengths = jnp.broadcast_to(lengths_ref[...], (8, lengths_ref.shape[1]))
    high = (lengths >> 5).astype(F32).astype(BF16)
    rest = (lengths & 31).astype(F32).astype(BF16)
    episode = lax.broadcasted_iota(jnp.int32, (lengths.shape[1], LANES), 0)
    lane = lax.broadcasted_iota(jnp.int32, (lengths.shape[1], LANES), 1)

    def total(chosen):
        picks = jnp.where(chosen, 1.0, 0.0).astype(BF16)
        return (32 * matmul(high, picks) + matmul(rest, picks)).astype(jnp.int32)

    row = lax.broadcasted_iota(jnp.int32, (8, LANES), 0)
    return jnp.where(row == 0, total(episode < lane), total(episode <= lane))


def project_kernel(
    count, lengths_ref, straight_ref, cross_a_ref, cross_b_ref, w_ref,
    q_x_ref, kv_x_ref, q_d_ref, kv_d_ref, give_ref, starts_x_ref, starts_d_ref, block_ref,
):
    place, side, core = where_am_i()
    group, width = block_ref.shape
    gather((cross_a_ref, cross_b_ref), block_ref)
    for normed, q_ref, kv_ref in (
        (block_ref[...], q_x_ref, kv_x_ref), (straight_ref[...], q_d_ref, kv_d_ref)
    ):
        q_ref[...] = (matmul(normed, w_ref[:, :width]) * SCALE2).astype(BF16)
        kv_ref[...] = matmul(normed, w_ref[:, width:]).astype(BF16)
    give_ref[:, 2 * width :] = block_ref[...]

    @pl.when(side == core)
    def _():
        give_ref[:, : 2 * width] = kv_d_ref[...]

    @pl.when(side != core)
    def _():
        give_ref[:, : 2 * width] = kv_x_ref[...]

    bounds = bounds_of(lengths_ref)
    fill_starts(starts_x_ref, bounds, block_first(1 - side, place, count, group))
    fill_starts(starts_d_ref, bounds, block_first(side, place, count, group))


def own_kernel(
    count, starts_x_ref, starts_d_ref, q_x_ref, kv_x_ref, q_d_ref, kv_d_ref,
    acc_x_ref, m_x_ref, acc_d_ref, m_d_ref,
):
    tiles = diagonal(q_x_ref.shape[0])
    place, side, _ = where_am_i()
    group = q_x_ref.shape[0]
    first = block_first(1 - side, place, count, group)
    keep(attend(q_x_ref, starts_x_ref, kv_x_ref, first, None, tiles), (acc_x_ref, m_x_ref))
    first = block_first(side, place, count, group)
    keep(attend(q_d_ref, starts_d_ref, kv_d_ref, first, None, tiles), (acc_d_ref, m_d_ref))


def partner_kernel(
    count, starts_x_ref, starts_d_ref, given_ref, q_x_ref, q_d_ref, acc_x_in, m_x_in, acc_d_in, m_d_in,
    acc_x_ref, m_x_ref, acc_d_ref, m_d_ref,
):
    place, side, core = where_am_i()
    group = q_x_ref.shape[0]
    half = 1 - core
    key_first = block_first(half, place, count, group) - group
    tiles = full(group)

    @pl.when(half == side)
    def _():
        out = attend(q_d_ref, starts_d_ref, given_ref, key_first, (acc_d_in, m_d_in), tiles)
        keep(out, (acc_d_ref, m_d_ref))
        acc_x_ref[...] = acc_x_in[...]
        m_x_ref[...] = m_x_in[...]

    @pl.when(half != side)
    def _():
        out = attend(q_x_ref, starts_x_ref, given_ref, key_first, (acc_x_in, m_x_in), tiles)
        keep(out, (acc_x_ref, m_x_ref))
        acc_d_ref[...] = acc_d_in[...]
        m_d_ref[...] = m_d_in[...]


def far_kernel(
    count, late, starts_ref, far_ref, given_ref, w_ref, q_ref, acc_in, m_in,
    acc_ref, m_ref, kv_ref, block_ref,
):
    place, side, _ = where_am_i()
    half = side if late else 1 - side
    group, width = far_ref.shape
    first = block_first(half, place, count, group)
    block_ref[...] = far_ref[...]
    if late:
        @pl.when(place // 2 == count // 2 - 1)
        def _():
            block_ref[...] = given_ref[:, 2 * width :]

    bare = (place < 2) if late else (place < 0)

    @pl.when(jnp.logical_not(bare))
    def _():
        kv_ref[...] = matmul(block_ref[...], w_ref[:, width:]).astype(BF16)
        out = attend(q_ref, starts_ref, kv_ref, first - 2 * group, (acc_in, m_in), beyond(group))
        keep(out, (acc_ref, m_ref))

    @pl.when(bare)
    def _():
        acc_ref[...] = acc_in[...]
        m_ref[...] = m_in[...]


def near_kernel(count, late, starts_ref, near_ref, cross_a_ref, cross_b_ref, *refs):
    w_ref, w_out_ref, q_ref, acc_in, m_in = refs[:5]
    out_ref, stage_ref, sems, kv_ref, block_ref = refs[-5:]
    place, side, core = where_am_i()
    half = side if late else 1 - side
    group, width = block_ref.shape
    first = block_first(half, place, count, group)
    rows = group // 2

    def emit(wide):
        for row in range(0, group, rows):
            rs = slice(row, row + rows)
            mixed = [(m[rs, :HEAD_DIM] / m[rs, HEAD_DIM:]).astype(BF16) for m in wide]
            out = matmul(jnp.concatenate(mixed, axis=1), w_out_ref[...])
            stage_ref[rs, :] = out.astype(BF16)
            copy_out(row).start()

    def copy_out(row):
        rs = pl.ds(row, rows)
        return pltpu.make_async_copy(
            stage_ref.at[rs], out_ref.at[0, half, rs], sems.at[row // rows]
        )

    wanted = half == core
    if late:
        wanted = wanted & (place >= 2)

    @pl.when(wanted)
    def _():
        block_ref[...] = near_ref[...]
        if late:
            @pl.when(place == count - 1)
            def _():
                gather((cross_a_ref, cross_b_ref), block_ref)

        kv_ref[...] = matmul(block_ref[...], w_ref[:, width:]).astype(BF16)
        out = attend(q_ref, starts_ref, kv_ref, first - group, (acc_in, m_in), full(group))
        emit([mixed for mixed, _ in out])

    @pl.when(jnp.logical_not(wanted))
    def _():
        emit([acc_in[:, h * WIDE : (h + 1) * WIDE] for h in range(HEADS)])

    for row in range(0, group, rows):
        copy_out(row).wait()


def params(mib):
    return pltpu.CompilerParams(vmem_limit_bytes=mib * 1024 * 1024)


def local(frames, episode_lengths, w_qkv, w_out):
    width = w_out.shape[0]
    group = frames.shape[2]
    count = lax.axis_size("ctx")
    chips = count // 2
    pair = [(i, i ^ 1) for i in range(count)]

    def route(links):
        return [(2 * a + c, 2 * b + c) for a, b in links for c in range(2)]

    even = [(c, c + 1) for c in range(0, chips - 1, 2)]
    odd = [(c, c + 1) for c in range(1, chips - 1, 2)]
    swap_x = route(even + [(b, a) for a, b in even])
    swap_d = route(odd + [(b, a) for a, b in odd])
    relay_out = route([(a, b + 1) for a, b in odd] + [(b, a - 1) for a, b in odd])
    relay_in = route([(b + 1, b) for a, b in odd] + [(a - 1, a) for a, b in odd])

    def send(block, links):
        return lax.ppermute(block, "ctx", links)

    def shape(*dims, dtype=BF16):
        return jax.ShapeDtypeStruct(dims, dtype)

    block = shape(group, width)
    part = shape(group // 2, width)
    kv_type = shape(group, 2 * width)
    state = (shape(group, HEADS * WIDE, dtype=F32), shape(group, width, dtype=F32))
    kv_scratch = [pltpu.VMEM((group, 2 * width), BF16), pltpu.VMEM((group, width), BF16)]

    def call(kernel, outs, operands, scratch=(), aliased=None):
        specs = [VMEM] * len(operands)
        options = dict(out_specs=(VMEM,) * len(outs), scratch_shapes=list(scratch))
        if aliased is not None:
            options["out_specs"] = (HBM,)
            options["scratch_shapes"] = [
                pltpu.VMEM((group, width), BF16), pltpu.SemaphoreType.DMA((2,)),
            ] + list(scratch)
        if aliased:
            specs.append(HBM)
            options["input_output_aliases"] = {len(operands): 0}
            operands = operands + aliased
        return pl.pallas_call(
            kernel,
            out_shape=outs,
            in_specs=specs,
            compiler_params=params(14),
            cost_estimate=pl.CostEstimate(flops=10**8, bytes_accessed=10**6, transcendentals=0),
            **options,
        )(*operands)

    straight, cross_a, cross_b = pl.pallas_call(
        prepare_kernel,
        out_shape=(block, part, part),
        in_specs=[VMEM],
        out_specs=(VMEM,) * 3,
        compiler_params=params(4),
        cost_estimate=pl.CostEstimate(flops=10**10, bytes_accessed=10**6, transcendentals=0),
    )(frames)
    x_in = send(straight, swap_x)
    hop_in = send(cross_a, relay_out)
    bind = functools.partial
    lengths = episode_lengths.reshape(1, -1)
    starts_type = shape(group, LANES, dtype=jnp.int32)
    q_x, kv_x, q_d, kv_d, give, starts_x, starts_d = call(
        bind(project_kernel, count),
        (block, kv_type, block, kv_type, shape(group, 3 * width), starts_type, starts_type),
        (lengths, straight, cross_a, cross_b, w_qkv), kv_scratch[1:],
    )
    d_in = send(cross_b, swap_d)
    given = send(give, pair)
    acc_x, m_x, acc_d, m_d = call(
        bind(own_kernel, count), state + state,
        (starts_x, starts_d, q_x, kv_x, q_d, kv_d),
    )
    hop_in, acc_x = lax.optimization_barrier((hop_in, acc_x))
    r_in = send(hop_in, relay_in)
    acc_x, m_x, acc_d, m_d = call(
        bind(partner_kernel, count), state + state,
        (starts_x, starts_d, given, q_x, q_d, acc_x, m_x, acc_d, m_d),
    )
    x_in, acc_d = lax.optimization_barrier((x_in, acc_d))
    near_x = send(x_in, pair)
    acc_x, m_x = call(
        bind(far_kernel, count, False), state,
        (starts_x, x_in, given, w_qkv, q_x, acc_x, m_x), kv_scratch,
    )
    whole = (jax.ShapeDtypeStruct(frames.shape, BF16),)
    (out,) = call(
        bind(near_kernel, count, False), whole,
        (starts_x, near_x, cross_a, cross_b, w_qkv, w_out, q_x, acc_x, m_x), kv_scratch, (),
    )
    r_in, d_in, out = lax.optimization_barrier((r_in, d_in, out))
    d_block = jnp.concatenate([r_in, d_in], axis=0)
    near_d = send(d_block, pair)
    acc_d, m_d = call(
        bind(far_kernel, count, True), state,
        (starts_d, d_block, given, w_qkv, q_d, acc_d, m_d), kv_scratch,
    )
    (out,) = call(
        bind(near_kernel, count, True), whole,
        (starts_d, near_d, cross_a, cross_b, w_qkv, w_out, q_d, acc_d, m_d), kv_scratch, (out,),
    )
    return out


def solution(mesh):
    in_specs = (P(("dp", "ctx"), None, None, None), P("dp"), P(), P())
    out_specs = P(("dp", "ctx"), None, None, None)
    return jax.shard_map(local, mesh=mesh, in_specs=in_specs, out_specs=out_specs, check_vma=False)
```

```python
import functools

import jax
import jax.numpy as jnp
from jax import lax
from jax.experimental import pallas as pl
from jax.experimental.pallas import tpu as pltpu
from jax.sharding import PartitionSpec as P


HEADS = 4
HEAD_DIM = 128
LANES = 128
WIDE = HEAD_DIM + LANES
SCALE2 = HEAD_DIM ** (-0.5) * 1.4426950408889634
APART = -1e30
VMEM = pl.BlockSpec(memory_space=pltpu.VMEM)
HBM = pl.BlockSpec(memory_space=pltpu.HBM)
F32 = jnp.float32
BF16 = jnp.bfloat16


def normalize(rows):
    wide = rows.astype(F32)
    factor = lax.rsqrt(jnp.mean(wide * wide, axis=-1, keepdims=True) + 1e-06)
    return (wide * factor).astype(BF16)


def matmul(left, right):
    return jnp.dot(left, right, preferred_element_type=F32)


def where_am_i():
    place = lax.axis_index("ctx")
    return place, lax.rem(place // 2, 2), lax.rem(place, 2)


def block_first(half, place, count, group):
    return jnp.where(half == 0, place, 2 * count - 1 - place) * group


def beside(left, right):
    return jnp.concatenate([left, right], axis=1)


def across(column, width):
    return jnp.concatenate([column] * (width // LANES), axis=1)


def inside(bounds, first, rows):
    position = first + lax.broadcasted_iota(jnp.int32, (rows, LANES), 0)
    return (position >= bounds[0:1, :]) & (position < bounds[1:2, :])


def fill_starts(starts_ref, bounds, first):
    rows = starts_ref.shape[0]
    chosen = jnp.where(inside(bounds, first, rows), bounds[0:1, :], 0)
    start = jnp.sum(chosen.astype(F32), axis=1, keepdims=True).astype(jnp.int32)
    starts_ref[...] = jnp.broadcast_to(start, starts_ref.shape)


def attend(q_ref, starts_ref, old, tiles, heads=range(HEADS)):
    rows, width = q_ref.shape
    out = []
    for head in heads:
        hs = pl.ds(head * HEAD_DIM, HEAD_DIM)
        vs = pl.ds(width + head * HEAD_DIM, HEAD_DIM)
        ws = pl.ds(head * WIDE, WIDE)
        scores, peaks = [], []
        for kv_ref, key_first, low, size, top, bottom, causal in tiles:
            tile = lax.dot_general(
                q_ref[pl.ds(top, bottom - top), hs],
                kv_ref[pl.ds(low, size), hs],
                (((1,), (1,)), ((), ())),
                preferred_element_type=F32,
            )
            reach = starts_ref[pl.ds(top, bottom - top), :] - (key_first + low)
            there = lax.broadcasted_iota(jnp.int32, tile.shape, 1)
            allowed = there >= across(reach, size)
            if causal:
                here = lax.broadcasted_iota(jnp.int32, tile.shape, 0)
                allowed = allowed & (there <= here)
            tile = jnp.where(allowed, tile, APART)
            scores.append(tile)
            peak = jnp.max(tile, axis=1, keepdims=True)
            peaks.append((jnp.broadcast_to(peak, (bottom - top, LANES)), top, bottom))
        peak = spread(jnp.maximum, peaks, rows)
        if old is not None:
            before = old[1][:, hs]
            peak = jnp.maximum(before, peak)
        mixes = []
        for tile, (kv_ref, _, low, size, top, bottom, _) in zip(scores, tiles):
            weights = jnp.exp2(tile - across(peak[top:bottom], size)).astype(BF16)
            ones = jnp.ones((size, LANES), BF16)
            mix = matmul(weights, beside(kv_ref[pl.ds(low, size), vs], ones))
            mixes.append((mix, top, bottom))
        mixed = spread(jnp.add, mixes, rows)
        if old is not None:
            mixed = mixed + across(jnp.exp2(before - peak), WIDE) * old[0][:, ws]
        out.append((mixed, peak))
    return out


def spread(combine, items, rows):
    whole = [item for item, top, bottom in items if bottom - top == rows]
    total = functools.reduce(combine, whole)
    for item, top, bottom in items:
        if bottom - top == rows:
            continue
        pieces = [total[:top]] if top else []
        pieces.append(combine(total[top:bottom], item))
        if bottom < rows:
            pieces.append(total[bottom:])
        total = jnp.concatenate(pieces, axis=0)
    return total


def keep(out, acc_ref, m_ref):
    for head, (mixed, peak) in enumerate(out):
        acc_ref[:, head * WIDE : (head + 1) * WIDE] = mixed
        m_ref[:, head * HEAD_DIM : (head + 1) * HEAD_DIM] = peak


def own_tiles(kv_ref, first):
    group = kv_ref.shape[0]
    rows = group // 2
    return [
        (kv_ref, first, 0, rows, 0, group, True),
        (kv_ref, first, rows, rows, rows, group, True),
    ]


def near_tiles(kv_ref, first):
    group = kv_ref.shape[0]
    return [(kv_ref, first - group, 0, group, 0, group, False)]


def far_tiles(kv_ref, first):
    group = kv_ref.shape[0]
    rows = group // 2
    return [
        (kv_ref, first - 2 * group, rows, rows, 0, group, False),
        (kv_ref, first - 2 * group, 0, rows, 0, rows, False),
    ]


def prepare_kernel(frames_ref, straight_ref, cross_a_ref, cross_b_ref):
    _, side, _ = where_am_i()
    straight_ref[...] = normalize(frames_ref[0, side])
    rows = cross_a_ref.shape[0]
    cross_a_ref[...] = normalize(frames_ref[0, 1 - side, :rows])
    cross_b_ref[...] = normalize(frames_ref[0, 1 - side, rows:])


def bounds_of(lengths_ref):
    lengths = jnp.broadcast_to(lengths_ref[...], (8, lengths_ref.shape[1]))
    high = (lengths >> 5).astype(F32).astype(BF16)
    rest = (lengths & 31).astype(F32).astype(BF16)
    episode = lax.broadcasted_iota(jnp.int32, (lengths.shape[1], LANES), 0)
    lane = lax.broadcasted_iota(jnp.int32, (lengths.shape[1], LANES), 1)

    def total(chosen):
        picks = jnp.where(chosen, 1.0, 0.0).astype(BF16)
        return (32 * matmul(high, picks) + matmul(rest, picks)).astype(jnp.int32)

    row = lax.broadcasted_iota(jnp.int32, (8, LANES), 0)
    return jnp.where(row == 0, total(episode < lane), total(episode <= lane))


def project_kernel(
    count, lengths_ref, straight_ref, cross_a_ref, cross_b_ref, w_ref,
    q_ref, give_ref, kv_ref, starts_ref, blocks_ref,
):
    place, side, core = where_am_i()
    _, group, width = blocks_ref.shape
    rows = cross_a_ref.shape[0]
    blocks_ref[side] = straight_ref[...]
    blocks_ref[1 - side, :rows] = cross_a_ref[...]
    blocks_ref[1 - side, rows:] = cross_b_ref[...]
    for half, pair_ref in ((core, give_ref), (1 - core, kv_ref)):
        normed = blocks_ref[half]
        pair_ref[...] = matmul(normed, w_ref[:, width:]).astype(BF16)
        q_ref[half] = (matmul(normed, w_ref[:, :width]) * SCALE2).astype(BF16)
    bounds = bounds_of(lengths_ref)
    for half in range(2):
        fill_starts(starts_ref.at[half], bounds, block_first(half, place, count, group))


def base_kernel(count, starts_ref, q_ref, give_ref, kv_ref, given_ref, acc_ref, m_ref):
    place, _, core = where_am_i()
    group = give_ref.shape[0]
    first = block_first(1 - core, place, count, group)
    tiles = own_tiles(kv_ref, first) + near_tiles(given_ref, first)
    out = attend(q_ref.at[1 - core], starts_ref.at[1 - core], None, tiles)
    keep(out, acc_ref.at[1 - core], m_ref.at[1 - core])
    first = block_first(core, place, count, group)
    out = attend(q_ref.at[core], starts_ref.at[core], None, own_tiles(give_ref, first))
    keep(out, acc_ref.at[core], m_ref.at[core])


def emitter(half, w_out_ref, out_ref, stage_ref, sems):
    group = stage_ref.shape[0]
    rows = group // 2

    def copy_out(row):
        rs = pl.ds(row, rows)
        return pltpu.make_async_copy(
            stage_ref.at[rs], out_ref.at[0, half, rs], sems.at[row // rows]
        )

    def emit(wide):
        for row in range(0, group, rows):
            rs = slice(row, row + rows)
            mixed = [(m[rs, :HEAD_DIM] / m[rs, HEAD_DIM:]).astype(BF16) for m in wide]
            out = matmul(jnp.concatenate(mixed, axis=1), w_out_ref[...])
            stage_ref[rs, :] = out.astype(BF16)
            copy_out(row).start()

    def settle():
        for row in range(0, group, rows):
            copy_out(row).wait()

    return emit, settle


def heads_of(acc_ref):
    return [acc_ref[:, h * WIDE : (h + 1) * WIDE] for h in range(HEADS)]


def merge_kernel(count, r_ref, d_ref, cross_a_ref, cross_b_ref, block_ref):
    place, _, _ = where_am_i()
    rows = r_ref.shape[0]
    at_end = place // 2 == count // 2 - 1

    @pl.when(at_end)
    def _():
        block_ref[:rows] = cross_a_ref[...]
        block_ref[rows:] = cross_b_ref[...]

    @pl.when(jnp.logical_not(at_end))
    def _():
        block_ref[:rows] = r_ref[...]
        block_ref[rows:] = d_ref[...]


def far_kernel(
    count, late, starts_ref, far_ref, given_ref, w_ref, w_out_ref, q_ref, acc_in, m_in, *refs
):
    acc_ref, m_ref, out_ref, stage_ref, sems, kv_ref = refs[-6:]
    place, side, core = where_am_i()
    half = side if late else 1 - side
    group, width = far_ref.shape
    first = block_first(half, place, count, group)
    emit, settle = emitter(half, w_out_ref, out_ref, stage_ref, sems)
    old = (acc_in.at[half], m_in.at[half])
    bare = late & (place < 2)
    waits = late & (place == count - 2)
    ends = late & (place == count - 1)
    idle = bare | waits
    emits = ((half != core) & jnp.logical_not(waits)) | bare

    @pl.when(jnp.logical_not(idle | ends))
    def _():
        kv_ref[...] = matmul(far_ref[...], w_ref[:, width:]).astype(BF16)

    if late:
        @pl.when(ends)
        def _():
            kv_ref[...] = given_ref[...]

    @pl.when(jnp.logical_not(idle))
    def _():
        out = attend(q_ref.at[half], starts_ref.at[half], old, far_tiles(kv_ref, first))
        keep(out, acc_ref, m_ref)

    if late:
        @pl.when(idle)
        def _():
            acc_ref[...] = old[0][...]
            m_ref[...] = old[1][...]

    @pl.when(emits)
    def _():
        emit(heads_of(acc_ref))
        settle()


def near_half_kernel(
    count, starts_ref, near_ref, w_ref, q_ref, acc_in, m_in, kv_ref, part_ref
):
    place, side, core = where_am_i()
    half = 1 - side
    group, width = near_ref.shape
    first = block_first(half, place, count, group)

    @pl.when(half == core)
    def _():
        kv_ref[...] = matmul(near_ref[...], w_ref[:, width:]).astype(BF16)
        out = attend(
            q_ref.at[half], starts_ref.at[half], (acc_in, m_in), near_tiles(kv_ref, first),
            range(HEADS // 2),
        )
        for head, (mixed, _) in enumerate(out):
            part_ref[:, head * WIDE : (head + 1) * WIDE] = mixed


def finish_x_kernel(
    count, starts_ref, kv_ref, part_ref, w_out_ref, q_ref, acc_in, m_in, whole_ref,
    out_ref, stage_ref, sems,
):
    place, side, core = where_am_i()
    half = 1 - side
    group = stage_ref.shape[0]
    first = block_first(half, place, count, group)
    emit, settle = emitter(half, w_out_ref, out_ref, stage_ref, sems)

    @pl.when(half == core)
    def _():
        out = attend(
            q_ref.at[half], starts_ref.at[half], (acc_in, m_in), near_tiles(kv_ref, first),
            range(HEADS // 2, HEADS),
        )
        done = [part_ref[:, h * WIDE : (h + 1) * WIDE] for h in range(HEADS // 2)]
        emit(done + [mixed for mixed, _ in out])
        settle()


def finish_d_kernel(
    count, starts_ref, near_ref, block_ref, w_ref, w_out_ref, q_ref, acc_in, m_in, whole_ref,
    out_ref, stage_ref, sems, kv_ref, source_ref,
):
    place, side, core = where_am_i()
    half = side
    group, width = near_ref.shape
    first = block_first(half, place, count, group)
    emit, settle = emitter(half, w_out_ref, out_ref, stage_ref, sems)
    waits = place == count - 2
    runs = ((half == core) & (place >= 2)) | waits

    @pl.when(runs)
    def _():
        source_ref[...] = near_ref[...]

        @pl.when(place == count - 1)
        def _():
            source_ref[...] = block_ref[...]

        kv_ref[...] = matmul(source_ref[...], w_ref[:, width:]).astype(BF16)
        tiles = near_tiles(kv_ref, first - jnp.where(waits, group, 0))
        out = attend(q_ref.at[half], starts_ref.at[half], (acc_in, m_in), tiles)
        emit([mixed for mixed, _ in out])
        settle()


def params(mib):
    return pltpu.CompilerParams(vmem_limit_bytes=mib * 1024 * 1024)


def local(frames, episode_lengths, w_qkv, w_out):
    width = w_out.shape[0]
    group = frames.shape[2]
    count = lax.axis_size("ctx")
    chips = count // 2
    pair = [(i, i ^ 1) for i in range(count)]

    def route(links):
        return [(2 * a + c, 2 * b + c) for a, b in links for c in range(2)]

    even = [(c, c + 1) for c in range(0, chips - 1, 2)]
    odd = [(c, c + 1) for c in range(1, chips - 1, 2)]
    swap_x = route(even + [(b, a) for a, b in even])
    swap_d = route(odd + [(b, a) for a, b in odd])
    relay_out = route([(a, b + 1) for a, b in odd] + [(b, a - 1) for a, b in odd])
    relay_in = route([(b + 1, b) for a, b in odd] + [(a - 1, a) for a, b in odd])

    def send(block, links):
        return lax.ppermute(block, "ctx", links)

    def shape(*dims, dtype=BF16):
        return jax.ShapeDtypeStruct(dims, dtype)

    block = shape(group, width)
    part = shape(group // 2, width)
    kv_type = shape(group, 2 * width)
    state = (shape(group, HEADS * WIDE, dtype=F32), shape(group, width, dtype=F32))
    states = tuple(shape(2, *s.shape, dtype=F32) for s in state)
    block_scratch = pltpu.VMEM(block.shape, BF16)
    kv_scratch = pltpu.VMEM(kv_type.shape, BF16)

    def call(kernel, outs, operands, scratch=(), writes=False, aliased=None):
        specs = [VMEM] * len(operands)
        out_specs = [VMEM] * len(outs)
        scratch = list(scratch)
        options = {}
        if writes:
            outs = tuple(outs) + (jax.ShapeDtypeStruct(frames.shape, BF16),)
            out_specs.append(HBM)
            scratch = [block_scratch, pltpu.SemaphoreType.DMA((2,))] + scratch
        if aliased is not None:
            specs.append(HBM)
            options["input_output_aliases"] = {len(operands): len(outs) - 1}
            operands = operands + (aliased,)
        return pl.pallas_call(
            functools.partial(kernel, count),
            out_shape=outs,
            in_specs=specs,
            out_specs=tuple(out_specs),
            scratch_shapes=scratch,
            compiler_params=params(14),
            cost_estimate=pl.CostEstimate(flops=10**8, bytes_accessed=10**6, transcendentals=0),
            **options,
        )(*operands)

    straight, cross_a, cross_b = pl.pallas_call(
        prepare_kernel,
        out_shape=(block, part, part),
        in_specs=[VMEM],
        out_specs=(VMEM,) * 3,
        compiler_params=params(4),
        cost_estimate=pl.CostEstimate(flops=10**10, bytes_accessed=10**6, transcendentals=0),
    )(frames)
    x_in = send(straight, swap_x)
    hop_in = send(cross_a, relay_out)
    lengths = episode_lengths.reshape(1, -1)
    q, give, kv, starts = call(
        project_kernel,
        (shape(2, group, width), kv_type, kv_type, shape(2, group, LANES, dtype=jnp.int32)),
        (lengths, straight, cross_a, cross_b, w_qkv), (pltpu.VMEM((2, group, width), BF16),),
    )
    given = send(give, pair)
    d_in = send(cross_b, swap_d)
    r_in = send(hop_in, relay_in)
    acc, m = call(base_kernel, states, (starts, q, give, kv, given))
    x_in, acc = lax.optimization_barrier((x_in, acc))
    near_x = send(x_in, pair)

    def far(count, *refs):
        return far_kernel(count, False, *refs)

    def far_late(count, *refs):
        return far_kernel(count, True, *refs)

    acc_x, m_x, out = call(
        far, state, (starts, x_in, given, w_qkv, w_out, q, acc, m), (kv_scratch,), True
    )
    kv_near, part_x = call(
        near_half_kernel, (kv_type, shape(group, HEADS // 2 * WIDE, dtype=F32)),
        (starts, near_x, w_qkv, q, acc_x, m_x),
    )
    r_in, d_in, part_x = lax.optimization_barrier((r_in, d_in, part_x))
    (d_block,) = call(merge_kernel, (block,), (r_in, d_in, cross_a, cross_b))
    near_d = send(d_block, pair)
    (out,) = call(
        finish_x_kernel, (), (starts, kv_near, part_x, w_out, q, acc_x, m_x),
        (), True, out,
    )
    acc_d, m_d, out = call(
        far_late, state, (starts, d_block, given, w_qkv, w_out, q, acc, m),
        (kv_scratch,), True, out,
    )
    (out,) = call(
        finish_d_kernel, (), (starts, near_d, d_block, w_qkv, w_out, q, acc_d, m_d),
        (kv_scratch, block_scratch), True, out,
    )
    return out


def solution(mesh):
    in_specs = (P(("dp", "ctx"), None, None, None), P("dp"), P(), P())
    out_specs = P(("dp", "ctx"), None, None, None)
    return jax.shard_map(local, mesh=mesh, in_specs=in_specs, out_specs=out_specs, check_vma=False)
```

```python
import functools

import jax
import jax.numpy as jnp
from jax import lax
from jax.experimental import pallas as pl
from jax.experimental.pallas import tpu as pltpu
from jax.sharding import PartitionSpec as P


HEADS = 4
HEAD_DIM = 128
LANES = 128
WIDE = HEAD_DIM + LANES
SCALE2 = HEAD_DIM ** (-0.5) * 1.4426950408889634
APART = -1e30
VMEM = pl.BlockSpec(memory_space=pltpu.VMEM)
HBM = pl.BlockSpec(memory_space=pltpu.HBM)
F32 = jnp.float32
BF16 = jnp.bfloat16


def normalize(rows):
    wide = rows.astype(F32)
    factor = lax.rsqrt(jnp.mean(wide * wide, axis=-1, keepdims=True) + 1e-06)
    return (wide * factor).astype(BF16)


def matmul(left, right):
    return jnp.dot(left, right, preferred_element_type=F32)


def where_am_i():
    place = lax.axis_index("ctx")
    return place, lax.rem(place // 2, 2), lax.rem(place, 2)


def block_first(half, place, count, group):
    return jnp.where(half == 0, place, 2 * count - 1 - place) * group


def beside(left, right):
    return jnp.concatenate([left, right], axis=1)


def across(column, width):
    return jnp.concatenate([column] * (width // LANES), axis=1)


def inside(bounds, first, rows):
    position = first + lax.broadcasted_iota(jnp.int32, (rows, LANES), 0)
    return (position >= bounds[0:1, :]) & (position < bounds[1:2, :])


def fill_starts(starts_ref, bounds, first):
    rows = starts_ref.shape[0]
    chosen = jnp.where(inside(bounds, first, rows), bounds[0:1, :], 0)
    start = jnp.sum(chosen.astype(F32), axis=1, keepdims=True).astype(jnp.int32)
    starts_ref[...] = jnp.broadcast_to(start, starts_ref.shape)


def attend(q_ref, starts_ref, old, tiles, heads=range(HEADS)):
    rows, width = q_ref.shape
    out = []
    for head in heads:
        hs = pl.ds(head * HEAD_DIM, HEAD_DIM)
        vs = pl.ds(width + head * HEAD_DIM, HEAD_DIM)
        ws = pl.ds(head * WIDE, WIDE)
        scores, peaks = [], []
        for kv_ref, key_first, low, size, top, bottom, causal in tiles:
            tile = lax.dot_general(
                q_ref[pl.ds(top, bottom - top), hs],
                kv_ref[pl.ds(low, size), hs],
                (((1,), (1,)), ((), ())),
                preferred_element_type=F32,
            )
            reach = starts_ref[pl.ds(top, bottom - top), :] - (key_first + low)
            there = lax.broadcasted_iota(jnp.int32, tile.shape, 1)
            allowed = there >= across(reach, size)
            if causal:
                here = lax.broadcasted_iota(jnp.int32, tile.shape, 0)
                allowed = allowed & (there <= here)
            tile = jnp.where(allowed, tile, APART)
            scores.append(tile)
            peak = jnp.max(tile, axis=1, keepdims=True)
            peaks.append((jnp.broadcast_to(peak, (bottom - top, LANES)), top, bottom))
        peak = spread(jnp.maximum, peaks, rows)
        if old is not None:
            before = old[1][:, hs]
            peak = jnp.maximum(before, peak)
        mixes = []
        for tile, (kv_ref, _, low, size, top, bottom, _) in zip(scores, tiles):
            weights = jnp.exp2(tile - across(peak[top:bottom], size)).astype(BF16)
            ones = jnp.ones((size, LANES), BF16)
            mix = matmul(weights, beside(kv_ref[pl.ds(low, size), vs], ones))
            mixes.append((mix, top, bottom))
        mixed = spread(jnp.add, mixes, rows)
        if old is not None:
            mixed = mixed + across(jnp.exp2(before - peak), WIDE) * old[0][:, ws]
        out.append((mixed, peak))
    return out


def spread(combine, items, rows):
    whole = [item for item, top, bottom in items if bottom - top == rows]
    total = functools.reduce(combine, whole)
    for item, top, bottom in items:
        if bottom - top == rows:
            continue
        pieces = [total[:top]] if top else []
        pieces.append(combine(total[top:bottom], item))
        if bottom < rows:
            pieces.append(total[bottom:])
        total = jnp.concatenate(pieces, axis=0)
    return total


def keep(out, acc_ref, m_ref):
    for head, (mixed, peak) in enumerate(out):
        acc_ref[:, head * WIDE : (head + 1) * WIDE] = mixed
        m_ref[:, head * HEAD_DIM : (head + 1) * HEAD_DIM] = peak


def own_tiles(kv_ref, first):
    group = kv_ref.shape[0]
    rows = group // 2
    return [
        (kv_ref, first, 0, rows, 0, group, True),
        (kv_ref, first, rows, rows, rows, group, True),
    ]


def near_tiles(kv_ref, first):
    group = kv_ref.shape[0]
    return [(kv_ref, first - group, 0, group, 0, group, False)]


def far_tiles(kv_ref, first):
    group = kv_ref.shape[0]
    rows = group // 2
    return [
        (kv_ref, first - 2 * group, rows, rows, 0, group, False),
        (kv_ref, first - 2 * group, 0, rows, 0, rows, False),
    ]


def prepare_kernel(frames_ref, straight_ref, other_ref, raw_ref, sems):
    _, side, _ = where_am_i()
    rows = raw_ref.shape[1]
    copies = []
    for index in range(2):
        piece = pl.ds(index * rows, rows)
        copies.append(
            pltpu.make_async_copy(frames_ref.at[0, side, piece], raw_ref.at[index], sems.at[index])
        )
    rest = pltpu.make_async_copy(frames_ref.at[0, 1 - side], other_ref, sems.at[2])
    for copy in copies:
        copy.start()
    rest.start()
    for index, copy in enumerate(copies):
        copy.wait()
        straight_ref[index * rows : (index + 1) * rows] = normalize(raw_ref[index])
    rest.wait()


def cross_kernel(count, other_ref, cross_a_ref, cross_b_ref):
    rows = cross_a_ref.shape[0]
    cross_a_ref[...] = normalize(other_ref[:rows])
    cross_b_ref[...] = normalize(other_ref[rows:])


def bounds_of(lengths_ref):
    lengths = jnp.broadcast_to(lengths_ref[...], (8, lengths_ref.shape[1]))
    high = (lengths >> 5).astype(F32).astype(BF16)
    rest = (lengths & 31).astype(F32).astype(BF16)
    episode = lax.broadcasted_iota(jnp.int32, (lengths.shape[1], LANES), 0)
    lane = lax.broadcasted_iota(jnp.int32, (lengths.shape[1], LANES), 1)

    def total(chosen):
        picks = jnp.where(chosen, 1.0, 0.0).astype(BF16)
        return (32 * matmul(high, picks) + matmul(rest, picks)).astype(jnp.int32)

    row = lax.broadcasted_iota(jnp.int32, (8, LANES), 0)
    return jnp.where(row == 0, total(episode < lane), total(episode <= lane))


def project_kernel(
    count, lengths_ref, straight_ref, cross_a_ref, cross_b_ref, w_ref,
    q_ref, give_ref, kv_ref, starts_ref, blocks_ref,
):
    place, side, core = where_am_i()
    _, group, width = blocks_ref.shape
    rows = cross_a_ref.shape[0]
    blocks_ref[side] = straight_ref[...]
    blocks_ref[1 - side, :rows] = cross_a_ref[...]
    blocks_ref[1 - side, rows:] = cross_b_ref[...]
    for half, pair_ref in ((core, give_ref), (1 - core, kv_ref)):
        normed = blocks_ref[half]
        pair_ref[...] = matmul(normed, w_ref[:, width:]).astype(BF16)
        q_ref[half] = (matmul(normed, w_ref[:, :width]) * SCALE2).astype(BF16)
    bounds = bounds_of(lengths_ref)
    for half in range(2):
        fill_starts(starts_ref.at[half], bounds, block_first(half, place, count, group))


def base_kernel(count, starts_ref, q_ref, give_ref, kv_ref, given_ref, acc_ref, m_ref):
    place, _, core = where_am_i()
    group = give_ref.shape[0]
    first = block_first(1 - core, place, count, group)
    tiles = own_tiles(kv_ref, first) + near_tiles(given_ref, first)
    out = attend(q_ref.at[1 - core], starts_ref.at[1 - core], None, tiles)
    keep(out, acc_ref.at[1 - core], m_ref.at[1 - core])
    first = block_first(core, place, count, group)
    out = attend(q_ref.at[core], starts_ref.at[core], None, own_tiles(give_ref, first))
    keep(out, acc_ref.at[core], m_ref.at[core])


def emitter(half, w_out_ref, out_ref, stage_ref, sems):
    group = stage_ref.shape[0]
    rows = group // 2

    def copy_out(row):
        rs = pl.ds(row, rows)
        return pltpu.make_async_copy(
            stage_ref.at[rs], out_ref.at[0, half, rs], sems.at[row // rows]
        )

    def emit(wide):
        for row in range(0, group, rows):
            rs = slice(row, row + rows)
            mixed = [(m[rs, :HEAD_DIM] / m[rs, HEAD_DIM:]).astype(BF16) for m in wide]
            out = matmul(jnp.concatenate(mixed, axis=1), w_out_ref[...])
            stage_ref[rs, :] = out.astype(BF16)
            copy_out(row).start()

    def settle():
        for row in range(0, group, rows):
            copy_out(row).wait()

    return emit, settle


def heads_of(acc_ref):
    return [acc_ref[:, h * WIDE : (h + 1) * WIDE] for h in range(HEADS)]


def merge_kernel(count, r_ref, d_ref, cross_a_ref, cross_b_ref, w_ref, kv_ref, block_ref):
    place, _, _ = where_am_i()
    rows = r_ref.shape[0]
    at_end = place // 2 == count // 2 - 1

    @pl.when(at_end)
    def _():
        block_ref[:rows] = cross_a_ref[...]
        block_ref[rows:] = cross_b_ref[...]

    @pl.when(jnp.logical_not(at_end))
    def _():
        block_ref[:rows] = r_ref[...]
        block_ref[rows:] = d_ref[...]

    width = block_ref.shape[1]

    @pl.when(place >= 2)
    def _():
        kv_ref[...] = matmul(block_ref[...], w_ref[:, width:]).astype(BF16)

    @pl.when(place < 2)
    def _():
        kv_ref[...] = jnp.zeros_like(kv_ref)


def far_x_kernel(
    count, starts_ref, far_ref, w_ref, w_out_ref, q_ref, acc_in, m_in,
    acc_ref, m_ref, out_ref, stage_ref, sems, kv_ref,
):
    place, side, core = where_am_i()
    half = 1 - side
    group, width = far_ref.shape
    first = block_first(half, place, count, group)
    emit, settle = emitter(half, w_out_ref, out_ref, stage_ref, sems)
    kv_ref[...] = matmul(far_ref[...], w_ref[:, width:]).astype(BF16)
    old = (acc_in.at[half], m_in.at[half])
    keep(attend(q_ref.at[half], starts_ref.at[half], old, far_tiles(kv_ref, first)), acc_ref, m_ref)

    @pl.when(half != core)
    def _():
        emit(heads_of(acc_ref))
        settle()


def far_d_kernel(
    count, starts_ref, far_ref, given_ref, w_out_ref, q_ref, acc_in, m_in, whole_ref,
    acc_ref, m_ref, out_ref, stage_ref, sems,
):
    place, side, core = where_am_i()
    half = side
    group = far_ref.shape[0]
    first = block_first(half, place, count, group)
    emit, settle = emitter(half, w_out_ref, out_ref, stage_ref, sems)
    old = (acc_in.at[half], m_in.at[half])
    bare = place < 2
    waits = place == count - 2
    idle = bare | waits

    ends = place == count - 1

    def run(kv_ref):
        out = attend(q_ref.at[half], starts_ref.at[half], old, far_tiles(kv_ref, first))
        keep(out, acc_ref, m_ref)

    @pl.when(jnp.logical_not(idle | ends))
    def _():
        run(far_ref)

    @pl.when(ends)
    def _():
        run(given_ref)

    @pl.when(idle)
    def _():
        acc_ref[...] = old[0][...]
        m_ref[...] = old[1][...]

    @pl.when(((half != core) & jnp.logical_not(waits)) | bare)
    def _():
        emit(heads_of(acc_ref))
        settle()


def near_half_kernel(
    count, starts_ref, near_ref, w_ref, q_ref, acc_in, m_in, kv_ref, part_ref
):
    place, side, core = where_am_i()
    half = 1 - side
    group, width = near_ref.shape
    first = block_first(half, place, count, group)

    @pl.when(half == core)
    def _():
        kv_ref[...] = matmul(near_ref[...], w_ref[:, width:]).astype(BF16)
        out = attend(
            q_ref.at[half], starts_ref.at[half], (acc_in, m_in), near_tiles(kv_ref, first),
            range(HEADS // 2),
        )
        for head, (mixed, _) in enumerate(out):
            part_ref[:, head * WIDE : (head + 1) * WIDE] = mixed


def finish_x_kernel(
    count, starts_ref, kv_ref, part_ref, w_out_ref, q_ref, acc_in, m_in, whole_ref,
    out_ref, stage_ref, sems,
):
    place, side, core = where_am_i()
    half = 1 - side
    group = stage_ref.shape[0]
    first = block_first(half, place, count, group)
    emit, settle = emitter(half, w_out_ref, out_ref, stage_ref, sems)

    @pl.when(half == core)
    def _():
        out = attend(
            q_ref.at[half], starts_ref.at[half], (acc_in, m_in), near_tiles(kv_ref, first),
            range(HEADS // 2, HEADS),
        )
        done = [part_ref[:, h * WIDE : (h + 1) * WIDE] for h in range(HEADS // 2)]
        emit(done + [mixed for mixed, _ in out])
        settle()


def finish_d_kernel(
    count, starts_ref, swapped_ref, kept_ref, w_out_ref, q_ref, acc_in, m_in, whole_ref,
    out_ref, stage_ref, sems,
):
    place, side, core = where_am_i()
    half = side
    group = swapped_ref.shape[0]
    first = block_first(half, place, count, group)
    emit, settle = emitter(half, w_out_ref, out_ref, stage_ref, sems)
    waits = place == count - 2
    ends = place == count - 1
    runs = ((half == core) & (place >= 2)) | waits

    def run(kv_ref):
        tiles = near_tiles(kv_ref, first - jnp.where(waits, group, 0))
        out = attend(q_ref.at[half], starts_ref.at[half], (acc_in, m_in), tiles)
        emit([mixed for mixed, _ in out])
        settle()

    @pl.when(runs & ends)
    def _():
        run(kept_ref)

    @pl.when(runs & jnp.logical_not(ends))
    def _():
        run(swapped_ref)


def params(mib):
    return pltpu.CompilerParams(vmem_limit_bytes=mib * 1024 * 1024)


def local(frames, episode_lengths, w_qkv, w_out):
    width = w_out.shape[0]
    group = frames.shape[2]
    count = lax.axis_size("ctx")
    chips = count // 2
    pair = [(i, i ^ 1) for i in range(count)]

    def route(links):
        return [(2 * a + c, 2 * b + c) for a, b in links for c in range(2)]

    even = [(c, c + 1) for c in range(0, chips - 1, 2)]
    odd = [(c, c + 1) for c in range(1, chips - 1, 2)]
    swap_x = route(even + [(b, a) for a, b in even])
    swap_d = route(odd + [(b, a) for a, b in odd])
    relay_out = route([(a, b + 1) for a, b in odd] + [(b, a - 1) for a, b in odd])
    relay_in = route([(b + 1, b) for a, b in odd] + [(a - 1, a) for a, b in odd])

    def send(block, links):
        return lax.ppermute(block, "ctx", links)

    def shape(*dims, dtype=BF16):
        return jax.ShapeDtypeStruct(dims, dtype)

    block = shape(group, width)
    part = shape(group // 2, width)
    kv_type = shape(group, 2 * width)
    state = (shape(group, HEADS * WIDE, dtype=F32), shape(group, width, dtype=F32))
    states = tuple(shape(2, *s.shape, dtype=F32) for s in state)
    block_scratch = pltpu.VMEM(block.shape, BF16)
    kv_scratch = pltpu.VMEM(kv_type.shape, BF16)

    def call(kernel, outs, operands, scratch=(), writes=False, aliased=None):
        specs = [VMEM] * len(operands)
        out_specs = [VMEM] * len(outs)
        scratch = list(scratch)
        options = {}
        if writes:
            outs = tuple(outs) + (jax.ShapeDtypeStruct(frames.shape, BF16),)
            out_specs.append(HBM)
            scratch = [block_scratch, pltpu.SemaphoreType.DMA((2,))] + scratch
        if aliased is not None:
            specs.append(HBM)
            options["input_output_aliases"] = {len(operands): len(outs) - 1}
            operands = operands + (aliased,)
        return pl.pallas_call(
            functools.partial(kernel, count),
            out_shape=outs,
            in_specs=specs,
            out_specs=tuple(out_specs),
            scratch_shapes=scratch,
            compiler_params=params(14),
            cost_estimate=pl.CostEstimate(flops=10**8, bytes_accessed=10**6, transcendentals=0),
            **options,
        )(*operands)

    straight, other = pl.pallas_call(
        prepare_kernel,
        out_shape=(block, block),
        in_specs=[HBM],
        out_specs=(VMEM,) * 2,
        scratch_shapes=[
            pltpu.VMEM((2, group // 2, width), BF16), pltpu.SemaphoreType.DMA((3,)),
        ],
        compiler_params=params(52),
        cost_estimate=pl.CostEstimate(flops=10**10, bytes_accessed=10**6, transcendentals=0),
    )(frames)
    x_in = send(straight, swap_x)
    cross_a, cross_b = call(cross_kernel, (part, part), (other,))
    hop_in = send(cross_a, relay_out)
    lengths = episode_lengths.reshape(1, -1)
    q, give, kv, starts = call(
        project_kernel,
        (shape(2, group, width), kv_type, kv_type, shape(2, group, LANES, dtype=jnp.int32)),
        (lengths, straight, cross_a, cross_b, w_qkv), (pltpu.VMEM((2, group, width), BF16),),
    )
    given = send(give, pair)
    d_in = send(cross_b, swap_d)
    r_in = send(hop_in, relay_in)
    acc, m = call(base_kernel, states, (starts, q, give, kv, given))
    x_in, acc = lax.optimization_barrier((x_in, acc))
    near_x = send(x_in, pair)
    acc_x, m_x, out = call(
        far_x_kernel, state, (starts, x_in, w_qkv, w_out, q, acc, m), (kv_scratch,), True
    )
    kv_near, part_x = call(
        near_half_kernel, (kv_type, shape(group, HEADS // 2 * WIDE, dtype=F32)),
        (starts, near_x, w_qkv, q, acc_x, m_x),
    )
    r_in, d_in, part_x = lax.optimization_barrier((r_in, d_in, part_x))
    (kv_d,) = call(
        merge_kernel, (kv_type,), (r_in, d_in, cross_a, cross_b, w_qkv), (block_scratch,)
    )
    near_d = send(kv_d, pair)
    (out,) = call(
        finish_x_kernel, (), (starts, kv_near, part_x, w_out, q, acc_x, m_x),
        (), True, out,
    )
    acc_d, m_d, out = call(
        far_d_kernel, state, (starts, kv_d, given, w_out, q, acc, m),
        (), True, out,
    )
    (out,) = call(
        finish_d_kernel, (), (starts, near_d, kv_d, w_out, q, acc_d, m_d),
        (), True, out,
    )
    return out


def solution(mesh):
    in_specs = (P(("dp", "ctx"), None, None, None), P("dp"), P(), P())
    out_specs = P(("dp", "ctx"), None, None, None)
    return jax.shard_map(local, mesh=mesh, in_specs=in_specs, out_specs=out_specs, check_vma=False)
```

```python
import functools

import jax
import jax.numpy as jnp
from jax import lax
from jax.experimental import pallas as pl
from jax.experimental.pallas import tpu as pltpu
from jax.sharding import PartitionSpec as P


HEADS = 4
HEAD_DIM = 128
LANES = 128
WIDE = HEAD_DIM + LANES
SCALE2 = HEAD_DIM ** (-0.5) * 1.4426950408889634
APART = -1e30
VMEM = pl.BlockSpec(memory_space=pltpu.VMEM)
HBM = pl.BlockSpec(memory_space=pltpu.HBM)
F32 = jnp.float32
BF16 = jnp.bfloat16


def normalize(rows):
    wide = rows.astype(F32)
    factor = lax.rsqrt(jnp.mean(wide * wide, axis=-1, keepdims=True) + 1e-06)
    return (wide * factor).astype(BF16)


def matmul(left, right):
    return jnp.dot(left, right, preferred_element_type=F32)


def where_am_i():
    place = lax.axis_index("ctx")
    return place, lax.rem(place // 2, 2), lax.rem(place, 2)


def block_first(half, place, count, group):
    return jnp.where(half == 0, place, 2 * count - 1 - place) * group


def beside(left, right):
    return jnp.concatenate([left, right], axis=1)


def across(column, width):
    return jnp.concatenate([column] * (width // LANES), axis=1)


def inside(bounds, first, rows):
    position = first + lax.broadcasted_iota(jnp.int32, (rows, LANES), 0)
    return (position >= bounds[0:1, :]) & (position < bounds[1:2, :])


def fill_starts(starts_ref, bounds, first):
    rows = starts_ref.shape[0]
    chosen = jnp.where(inside(bounds, first, rows), bounds[0:1, :], 0)
    start = jnp.sum(chosen.astype(F32), axis=1, keepdims=True).astype(jnp.int32)
    starts_ref[...] = jnp.broadcast_to(start, starts_ref.shape)


def attend(q_ref, starts_ref, old, tiles, heads=range(HEADS)):
    rows, width = q_ref.shape
    out = []
    for head in heads:
        hs = pl.ds(head * HEAD_DIM, HEAD_DIM)
        vs = pl.ds(width + head * HEAD_DIM, HEAD_DIM)
        ws = pl.ds(head * WIDE, WIDE)
        scores, peaks = [], []
        for kv_ref, key_first, low, size, top, bottom, causal in tiles:
            tile = lax.dot_general(
                q_ref[pl.ds(top, bottom - top), hs],
                kv_ref[pl.ds(low, size), hs],
                (((1,), (1,)), ((), ())),
                preferred_element_type=F32,
            )
            reach = starts_ref[pl.ds(top, bottom - top), :] - (key_first + low)
            there = lax.broadcasted_iota(jnp.int32, tile.shape, 1)
            allowed = there >= across(reach, size)
            if causal:
                here = lax.broadcasted_iota(jnp.int32, tile.shape, 0)
                allowed = allowed & (there <= here)
            tile = jnp.where(allowed, tile, APART)
            scores.append(tile)
            peak = jnp.max(tile, axis=1, keepdims=True)
            peaks.append((jnp.broadcast_to(peak, (bottom - top, LANES)), top, bottom))
        peak = spread(jnp.maximum, peaks, rows)
        if old is not None:
            before = old[1][:, hs]
            peak = jnp.maximum(before, peak)
        mixes = []
        for tile, (kv_ref, _, low, size, top, bottom, _) in zip(scores, tiles):
            weights = jnp.exp2((tile - across(peak[top:bottom], size)) * SCALE2).astype(BF16)
            ones = jnp.ones((size, LANES), BF16)
            mix = matmul(weights, beside(kv_ref[pl.ds(low, size), vs], ones))
            mixes.append((mix, top, bottom))
        mixed = spread(jnp.add, mixes, rows)
        if old is not None:
            mixed = mixed + across(jnp.exp2((before - peak) * SCALE2), WIDE) * old[0][:, ws]
        out.append((mixed, peak))
    return out


def spread(combine, items, rows):
    whole = [item for item, top, bottom in items if bottom - top == rows]
    total = functools.reduce(combine, whole)
    for item, top, bottom in items:
        if bottom - top == rows:
            continue
        pieces = [total[:top]] if top else []
        pieces.append(combine(total[top:bottom], item))
        if bottom < rows:
            pieces.append(total[bottom:])
        total = jnp.concatenate(pieces, axis=0)
    return total


def keep(out, acc_ref, m_ref):
    for head, (mixed, peak) in enumerate(out):
        acc_ref[:, head * WIDE : (head + 1) * WIDE] = mixed
        m_ref[:, head * HEAD_DIM : (head + 1) * HEAD_DIM] = peak


def own_tiles(kv_ref, first):
    group = kv_ref.shape[0]
    rows = group // 2
    return [
        (kv_ref, first, 0, rows, 0, group, True),
        (kv_ref, first, rows, rows, rows, group, True),
    ]


def near_tiles(kv_ref, first):
    group = kv_ref.shape[0]
    return [(kv_ref, first - group, 0, group, 0, group, False)]


def far_tiles(kv_ref, first):
    group = kv_ref.shape[0]
    rows = group // 2
    return [
        (kv_ref, first - 2 * group, rows, rows, 0, group, False),
        (kv_ref, first - 2 * group, 0, rows, 0, rows, False),
    ]


def prepare_kernel(frames_ref, straight_ref, other_ref, raw_ref, sems):
    _, side, _ = where_am_i()
    rows = raw_ref.shape[1]
    copies = []
    for index in range(2):
        piece = pl.ds(index * rows, rows)
        copies.append(
            pltpu.make_async_copy(frames_ref.at[0, side, piece], raw_ref.at[index], sems.at[index])
        )
    rest = pltpu.make_async_copy(frames_ref.at[0, 1 - side], other_ref, sems.at[2])
    for copy in copies:
        copy.start()
    rest.start()
    for index, copy in enumerate(copies):
        copy.wait()
        straight_ref[index * rows : (index + 1) * rows] = normalize(raw_ref[index])
    rest.wait()


def cross_kernel(count, other_ref, cross_a_ref, cross_b_ref):
    rows = cross_a_ref.shape[0]
    cross_a_ref[...] = normalize(other_ref[:rows])
    cross_b_ref[...] = normalize(other_ref[rows:])


def bounds_of(lengths_ref):
    lengths = jnp.broadcast_to(lengths_ref[...], (8, lengths_ref.shape[1]))
    high = (lengths >> 5).astype(F32).astype(BF16)
    rest = (lengths & 31).astype(F32).astype(BF16)
    episode = lax.broadcasted_iota(jnp.int32, (lengths.shape[1], LANES), 0)
    lane = lax.broadcasted_iota(jnp.int32, (lengths.shape[1], LANES), 1)

    def total(chosen):
        picks = jnp.where(chosen, 1.0, 0.0).astype(BF16)
        return (32 * matmul(high, picks) + matmul(rest, picks)).astype(jnp.int32)

    row = lax.broadcasted_iota(jnp.int32, (8, LANES), 0)
    return jnp.where(row == 0, total(episode < lane), total(episode <= lane))


def project_kernel(
    count, lengths_ref, straight_ref, cross_a_ref, cross_b_ref, w_ref,
    q_ref, give_ref, kv_ref, starts_ref, blocks_ref,
):
    place, side, core = where_am_i()
    _, group, width = blocks_ref.shape
    rows = cross_a_ref.shape[0]
    blocks_ref[side] = straight_ref[...]
    blocks_ref[1 - side, :rows] = cross_a_ref[...]
    blocks_ref[1 - side, rows:] = cross_b_ref[...]
    for half, pair_ref in ((core, give_ref), (1 - core, kv_ref)):
        normed = blocks_ref[half]
        pair_ref[...] = matmul(normed, w_ref[:, width:]).astype(BF16)
        q_ref[half] = matmul(normed, w_ref[:, :width]).astype(BF16)
    bounds = bounds_of(lengths_ref)
    for half in range(2):
        fill_starts(starts_ref.at[half], bounds, block_first(half, place, count, group))


def base_kernel(count, starts_ref, q_ref, give_ref, kv_ref, given_ref, acc_ref, m_ref):
    place, _, core = where_am_i()
    group = give_ref.shape[0]
    first = block_first(1 - core, place, count, group)
    tiles = own_tiles(kv_ref, first) + near_tiles(given_ref, first)
    out = attend(q_ref.at[1 - core], starts_ref.at[1 - core], None, tiles)
    keep(out, acc_ref.at[1 - core], m_ref.at[1 - core])
    first = block_first(core, place, count, group)
    out = attend(q_ref.at[core], starts_ref.at[core], None, own_tiles(give_ref, first))
    keep(out, acc_ref.at[core], m_ref.at[core])


def emitter(half, w_out_ref, out_ref, stage_ref, sems):
    group = stage_ref.shape[0]
    rows = group // 2

    def copy_out(row):
        rs = pl.ds(row, rows)
        return pltpu.make_async_copy(
            stage_ref.at[rs], out_ref.at[0, half, rs], sems.at[row // rows]
        )

    def emit(wide):
        for row in range(0, group, rows):
            rs = slice(row, row + rows)
            mixed = [(m[rs, :HEAD_DIM] / m[rs, HEAD_DIM:]).astype(BF16) for m in wide]
            out = matmul(jnp.concatenate(mixed, axis=1), w_out_ref[...])
            stage_ref[rs, :] = out.astype(BF16)
            copy_out(row).start()

    def settle():
        for row in range(0, group, rows):
            copy_out(row).wait()

    return emit, settle


def heads_of(acc_ref):
    return [acc_ref[:, h * WIDE : (h + 1) * WIDE] for h in range(HEADS)]


def merge_kernel(count, r_ref, d_ref, cross_a_ref, cross_b_ref, w_ref, kv_ref, block_ref):
    place, _, _ = where_am_i()
    rows = r_ref.shape[0]
    at_end = place // 2 == count // 2 - 1

    @pl.when(at_end)
    def _():
        block_ref[:rows] = cross_a_ref[...]
        block_ref[rows:] = cross_b_ref[...]

    @pl.when(jnp.logical_not(at_end))
    def _():
        block_ref[:rows] = r_ref[...]
        block_ref[rows:] = d_ref[...]

    width = block_ref.shape[1]

    @pl.when(place >= 2)
    def _():
        kv_ref[...] = matmul(block_ref[...], w_ref[:, width:]).astype(BF16)

    @pl.when(place < 2)
    def _():
        kv_ref[...] = jnp.zeros_like(kv_ref)


def far_x_kernel(
    count, starts_ref, far_ref, w_ref, w_out_ref, q_ref, acc_in, m_in,
    acc_ref, m_ref, out_ref, stage_ref, sems, kv_ref,
):
    place, side, core = where_am_i()
    half = 1 - side
    group, width = far_ref.shape
    first = block_first(half, place, count, group)
    emit, settle = emitter(half, w_out_ref, out_ref, stage_ref, sems)
    kv_ref[...] = matmul(far_ref[...], w_ref[:, width:]).astype(BF16)
    old = (acc_in.at[half], m_in.at[half])
    keep(attend(q_ref.at[half], starts_ref.at[half], old, far_tiles(kv_ref, first)), acc_ref, m_ref)

    @pl.when(half != core)
    def _():
        emit(heads_of(acc_ref))
        settle()


def far_d_kernel(
    count, starts_ref, far_ref, given_ref, w_out_ref, q_ref, acc_in, m_in, whole_ref,
    acc_ref, m_ref, out_ref, stage_ref, sems,
):
    place, side, core = where_am_i()
    half = side
    group = far_ref.shape[0]
    first = block_first(half, place, count, group)
    emit, settle = emitter(half, w_out_ref, out_ref, stage_ref, sems)
    old = (acc_in.at[half], m_in.at[half])
    bare = place < 2
    waits = place == count - 2
    idle = bare | waits

    ends = place == count - 1

    def run(kv_ref):
        out = attend(q_ref.at[half], starts_ref.at[half], old, far_tiles(kv_ref, first))
        keep(out, acc_ref, m_ref)

    @pl.when(jnp.logical_not(idle | ends))
    def _():
        run(far_ref)

    @pl.when(ends)
    def _():
        run(given_ref)

    @pl.when(idle)
    def _():
        acc_ref[...] = old[0][...]
        m_ref[...] = old[1][...]

    @pl.when(((half != core) & jnp.logical_not(waits)) | bare)
    def _():
        emit(heads_of(acc_ref))
        settle()


def near_half_kernel(
    count, starts_ref, near_ref, w_ref, q_ref, acc_in, m_in, kv_ref, part_ref
):
    place, side, core = where_am_i()
    half = 1 - side
    group, width = near_ref.shape
    first = block_first(half, place, count, group)

    @pl.when(half == core)
    def _():
        kv_ref[...] = matmul(near_ref[...], w_ref[:, width:]).astype(BF16)
        out = attend(
            q_ref.at[half], starts_ref.at[half], (acc_in, m_in), near_tiles(kv_ref, first),
            range(HEADS // 2),
        )
        for head, (mixed, _) in enumerate(out):
            part_ref[:, head * WIDE : (head + 1) * WIDE] = mixed


def finish_x_kernel(
    count, starts_ref, kv_ref, part_ref, w_out_ref, q_ref, acc_in, m_in, whole_ref,
    out_ref, stage_ref, sems,
):
    place, side, core = where_am_i()
    half = 1 - side
    group = stage_ref.shape[0]
    first = block_first(half, place, count, group)
    emit, settle = emitter(half, w_out_ref, out_ref, stage_ref, sems)

    @pl.when(half == core)
    def _():
        out = attend(
            q_ref.at[half], starts_ref.at[half], (acc_in, m_in), near_tiles(kv_ref, first),
            range(HEADS // 2, HEADS),
        )
        done = [part_ref[:, h * WIDE : (h + 1) * WIDE] for h in range(HEADS // 2)]
        emit(done + [mixed for mixed, _ in out])
        settle()


def finish_d_kernel(
    count, starts_ref, swapped_ref, kept_ref, w_out_ref, q_ref, acc_in, m_in, whole_ref,
    out_ref, stage_ref, sems,
):
    place, side, core = where_am_i()
    half = side
    group = swapped_ref.shape[0]
    first = block_first(half, place, count, group)
    emit, settle = emitter(half, w_out_ref, out_ref, stage_ref, sems)
    waits = place == count - 2
    ends = place == count - 1
    runs = ((half == core) & (place >= 2)) | waits

    def run(kv_ref):
        tiles = near_tiles(kv_ref, first - jnp.where(waits, group, 0))
        out = attend(q_ref.at[half], starts_ref.at[half], (acc_in, m_in), tiles)
        emit([mixed for mixed, _ in out])
        settle()

    @pl.when(runs & ends)
    def _():
        run(kept_ref)

    @pl.when(runs & jnp.logical_not(ends))
    def _():
        run(swapped_ref)


def params(mib):
    return pltpu.CompilerParams(vmem_limit_bytes=mib * 1024 * 1024)


def local(frames, episode_lengths, w_qkv, w_out):
    width = w_out.shape[0]
    group = frames.shape[2]
    count = lax.axis_size("ctx")
    chips = count // 2
    pair = [(i, i ^ 1) for i in range(count)]

    def route(links):
        return [(2 * a + c, 2 * b + c) for a, b in links for c in range(2)]

    even = [(c, c + 1) for c in range(0, chips - 1, 2)]
    odd = [(c, c + 1) for c in range(1, chips - 1, 2)]
    swap_x = route(even + [(b, a) for a, b in even])
    swap_d = route(odd + [(b, a) for a, b in odd])
    relay_out = route([(a, b + 1) for a, b in odd] + [(b, a - 1) for a, b in odd])
    relay_in = route([(b + 1, b) for a, b in odd] + [(a - 1, a) for a, b in odd])

    def send(block, links):
        return lax.ppermute(block, "ctx", links)

    def shape(*dims, dtype=BF16):
        return jax.ShapeDtypeStruct(dims, dtype)

    block = shape(group, width)
    part = shape(group // 2, width)
    kv_type = shape(group, 2 * width)
    state = (shape(group, HEADS * WIDE, dtype=F32), shape(group, width, dtype=F32))
    states = tuple(shape(2, *s.shape, dtype=F32) for s in state)
    block_scratch = pltpu.VMEM(block.shape, BF16)
    kv_scratch = pltpu.VMEM(kv_type.shape, BF16)

    def call(kernel, outs, operands, scratch=(), writes=False, aliased=None):
        specs = [VMEM] * len(operands)
        out_specs = [VMEM] * len(outs)
        scratch = list(scratch)
        options = {}
        if writes:
            outs = tuple(outs) + (jax.ShapeDtypeStruct(frames.shape, BF16),)
            out_specs.append(HBM)
            scratch = [block_scratch, pltpu.SemaphoreType.DMA((2,))] + scratch
        if aliased is not None:
            specs.append(HBM)
            options["input_output_aliases"] = {len(operands): len(outs) - 1}
            operands = operands + (aliased,)
        return pl.pallas_call(
            functools.partial(kernel, count),
            out_shape=outs,
            in_specs=specs,
            out_specs=tuple(out_specs),
            scratch_shapes=scratch,
            compiler_params=params(14),
            cost_estimate=pl.CostEstimate(flops=10**8, bytes_accessed=10**6, transcendentals=0),
            **options,
        )(*operands)

    straight, other = pl.pallas_call(
        prepare_kernel,
        out_shape=(block, block),
        in_specs=[HBM],
        out_specs=(VMEM,) * 2,
        scratch_shapes=[
            pltpu.VMEM((2, group // 2, width), BF16), pltpu.SemaphoreType.DMA((3,)),
        ],
        compiler_params=params(52),
        cost_estimate=pl.CostEstimate(flops=10**10, bytes_accessed=10**6, transcendentals=0),
    )(frames)
    x_in = send(straight, swap_x)
    cross_a, cross_b = call(cross_kernel, (part, part), (other,))
    hop_in = send(cross_a, relay_out)
    lengths = episode_lengths.reshape(1, -1)
    q, give, kv, starts = call(
        project_kernel,
        (shape(2, group, width), kv_type, kv_type, shape(2, group, LANES, dtype=jnp.int32)),
        (lengths, straight, cross_a, cross_b, w_qkv), (pltpu.VMEM((2, group, width), BF16),),
    )
    given = send(give, pair)
    d_in = send(cross_b, swap_d)
    r_in = send(hop_in, relay_in)
    acc, m = call(base_kernel, states, (starts, q, give, kv, given))
    x_in, acc = lax.optimization_barrier((x_in, acc))
    near_x = send(x_in, pair)
    acc_x, m_x, out = call(
        far_x_kernel, state, (starts, x_in, w_qkv, w_out, q, acc, m), (kv_scratch,), True
    )
    kv_near, part_x = call(
        near_half_kernel, (kv_type, shape(group, HEADS // 2 * WIDE, dtype=F32)),
        (starts, near_x, w_qkv, q, acc_x, m_x),
    )
    r_in, d_in, part_x = lax.optimization_barrier((r_in, d_in, part_x))
    (kv_d,) = call(
        merge_kernel, (kv_type,), (r_in, d_in, cross_a, cross_b, w_qkv), (block_scratch,)
    )
    near_d = send(kv_d, pair)
    (out,) = call(
        finish_x_kernel, (), (starts, kv_near, part_x, w_out, q, acc_x, m_x),
        (), True, out,
    )
    acc_d, m_d, out = call(
        far_d_kernel, state, (starts, kv_d, given, w_out, q, acc, m),
        (), True, out,
    )
    (out,) = call(
        finish_d_kernel, (), (starts, near_d, kv_d, w_out, q, acc_d, m_d),
        (), True, out,
    )
    return out


def solution(mesh):
    in_specs = (P(("dp", "ctx"), None, None, None), P("dp"), P(), P())
    out_specs = P(("dp", "ctx"), None, None, None)
    return jax.shard_map(local, mesh=mesh, in_specs=in_specs, out_specs=out_specs, check_vma=False)
```
